128 devices in a mesh: blk: 16 (over y, x), win: 8 (over z, core).
Axes of the slice: x: 4, y: 4, z: 4, core: 2. Of those that a mesh axis runs over, the one named last changes fastest.
Arguments:
- record: bfloat16 [16384, 8192], P('blk', 'win'), may hold values from -6 to 6
- deck_ids: int32 [128], replicated, may hold values from 0 to 1, as said below
- partners: int32 [128, 4], replicated, may hold values from 0 to 127, as said below
Outputs:
- correlations: bfloat16 [512, 64, 16384], P(('blk', 'win'))
The draws below stay inside these ranges and needn't reach their ends.
Inputs may be any that keep to these rules, and one draw needn't show every extreme that they name: `deck_ids`: 0 on the first deck and 1 on the second; non-decreasing in the block id (a single switch from 0 to 1), and both decks occur. Row b lists the partner blocks of block b. Take the blocks in groups of 8 consecutive ids: the partners of the blocks of one group are all different, and they name exactly 2 blocks of every group.
All inputs are finite; a program needn't handle non-finite values.
Results may differ from the reference program's by a relative error of at most 0.0075.
Values may be sent and summed in bfloat16 or wider, within the bound.
No kernel may reach another device: no remote copies, remote signals or barrier semaphores. Data moves between devices by JAX's collectives and lax.ppermute only.
A program may use at most 128 MiB of HBM per device.

```python
import math
import jax
import jax.numpy as jnp
from jax import lax

BCH = 128
WS = 512
BINS = 128
LAGS = 64
PAIR_DEV = 4
WINDOWS = 16
SAMPLES = 8192
BLOCKS = 128
CHANNELS = 16384
PAIRS = 512
CAP = 2
N_BLK = 16
N_WIN = 8


def draw_deck_ids(key, part):
    deck_key = jax.random.fold_in(key, 7)
    boundary = jax.random.randint(deck_key, (), BLOCKS // 4, 3 * BLOCKS // 4 + 1)
    return (jnp.arange(BLOCKS, dtype=jnp.int32) >= boundary).astype(jnp.int32)


def draw_partners(key, part):
    pick_key = jax.random.fold_in(key, 11)
    order_key = jax.random.fold_in(key, 13)
    scores = jax.random.randint(pick_key, (N_BLK, N_BLK, N_WIN), 0, 1 << 20) * N_WIN + jnp.arange(N_WIN, dtype=jnp.int32)
    picked = jnp.argsort(scores, axis=-1)[:, :, :CAP]
    chosen_blocks = (jnp.arange(N_BLK, dtype=jnp.int32)[None, :, None] * N_WIN + picked).reshape(N_BLK, N_BLK * CAP)
    spread = N_BLK * CAP
    shuffle = jax.random.randint(order_key, (N_BLK, spread), 0, 1 << 20) * spread + jnp.arange(spread, dtype=jnp.int32)
    placing = jnp.argsort(shuffle, axis=-1)
    mixed = jnp.take_along_axis(chosen_blocks, placing, axis=-1)
    return mixed.reshape(BLOCKS, PAIR_DEV).astype(jnp.int32)


def block_scale(key, dims, split, smallest, top_value):
    level, own = 1.0, jax.random.fold_in(key, 6)
    for axis_at, shards_of in split:
        heights = jnp.exp(jax.random.uniform(jax.random.fold_in(own, axis_at), (shards_of,), jnp.float32, smallest / len(split), top_value / len(split)))
        level = level * jnp.repeat(heights, dims[axis_at] // shards_of).reshape([-1 if axis == axis_at else 1 for axis in range(len(dims))])
    return level


def scatter_about(rng, dims, deviation, reach, pieces=(), kind=jnp.bfloat16):
    loudness = block_scale(rng, dims, pieces, -0.22, 0.18) if pieces else 1.0
    array = jax.random.normal(rng, dims, jnp.float32) * deviation * loudness
    return jnp.minimum(jnp.maximum(array, -reach), reach).astype(kind)


def setup_inputs(seed: int = 0) -> dict:
    key_of = jax.random.split(jax.random.key(seed), 4)
    return {
        "record": scatter_about(key_of[0], (CHANNELS, SAMPLES), 1.0, 6.0, ((0, 16), (1, 8))),
        "deck_ids": draw_deck_ids(jax.random.fold_in(key_of[3], 71), 0),
        "partners": draw_partners(jax.random.fold_in(key_of[3], 71), 0),
    }


def forward_table():
    samples = jnp.arange(WS, dtype=jnp.int32)
    frequency = jnp.arange(1, BINS + 1, dtype=jnp.int32)
    phases = samples[:, None] * frequency[None, :] % WS
    angles = phases.astype(jnp.float32) * (2.0 * math.pi / WS)
    return jnp.concatenate([jnp.cos(angles), -jnp.sin(angles)], axis=1).astype(jnp.bfloat16)

def inverse_table():
    frequency = jnp.arange(1, BINS + 1, dtype=jnp.int32)
    shifts = jnp.arange(LAGS, dtype=jnp.int32) - LAGS // 2
    phases = frequency[:, None] * shifts[None, :] % WS
    angles = phases.astype(jnp.float32) * (2.0 * math.pi / WS)
    return jnp.stack([jnp.cos(angles), -jnp.sin(angles)], axis=0).astype(jnp.bfloat16)

def whiten(windowed, polarity):
    spectra = jnp.dot(windowed, forward_table(), preferred_element_type=jnp.float32)
    power_mean = lax.optimization_barrier(jnp.sum(spectra * spectra, axis=1)) / BINS
    factor = polarity / jnp.sqrt(power_mean + 1e-06)
    return (spectra * factor[:, None]).astype(jnp.bfloat16)

def correlate(own_block, partner, inverse):
    own_values = own_block.reshape(BCH, WINDOWS, 2, BINS).astype(jnp.float32)
    partner_values = partner.reshape(BCH, WINDOWS, 2, BINS).astype(jnp.float32)
    rotated = jnp.stack([own_values[:, :, 1], -own_values[:, :, 0]], axis=2)
    real_part = jnp.einsum('iwcf,jwcf->fij', own_values, partner_values)
    imag_part = jnp.einsum('iwcf,jwcf->fij', rotated, partner_values)
    cross_spec = jnp.stack([real_part, imag_part], axis=1).astype(jnp.bfloat16)
    lagged = jnp.einsum('fvij,vfl->lij', cross_spec.astype(jnp.float32), inverse.astype(jnp.float32))
    lag_scale = 1.0 / math.sqrt(WINDOWS * BINS)
    return (lagged * lag_scale).reshape(LAGS, BCH * BCH).astype(jnp.bfloat16)

def reference(record, deck_ids, partners):
    polarity = jnp.repeat(1.0 - 2.0 * deck_ids.astype(jnp.float32), BCH * WINDOWS)
    whitened = whiten(record.reshape(CHANNELS * WINDOWS, WS), polarity)
    blocks = whitened.reshape(BLOCKS, BCH, WINDOWS, 2 * BINS)
    inverse = inverse_table()
    flat_partners = partners.reshape(-1)

    def one_pair(pair_index):
        own_block = lax.dynamic_index_in_dim(blocks, pair_index // PAIR_DEV, 0, keepdims=False)
        partner = lax.dynamic_index_in_dim(blocks, flat_partners[pair_index], 0, keepdims=False)
        return correlate(own_block, partner, inverse)
    return lax.map(one_pair, jnp.arange(PAIRS, dtype=jnp.int32))
```

```python
import functools
import math

import jax
import jax.numpy as jnp
import ml_dtypes
import numpy as np
from jax import lax
from jax.experimental import pallas as pl
from jax.experimental.pallas import tpu as pltpu
from jax.sharding import PartitionSpec as P

WS = 512
BINS = 128
LAGS = 64
BCH = 128
OCT = BINS // 8
ROWS = OCT * 32
CHUNKS = 1
VMEM_LIMIT = 56 * 1024 * 1024


def forward_table():
    t = np.arange(WS)
    f = np.arange(1, BINS + 1)
    angle = (f[:, None] * t[None, :] % WS) * (2.0 * math.pi / WS)
    return np.concatenate([np.cos(angle), -np.sin(angle)], 0).astype(ml_dtypes.bfloat16)


def lag_table():
    f = np.arange(1, BINS + 1)
    s = np.arange(LAGS) - LAGS // 2
    angle = (s[:, None] * f[None, :] % WS) * (2.0 * math.pi / WS)
    both = np.stack([np.cos(angle), -np.sin(angle)], 1).reshape(LAGS, 2, OCT, 8)
    return both.transpose(0, 2, 1, 3).reshape(LAGS, 2 * BINS).astype(ml_dtypes.bfloat16)


def spread_table():
    i = np.arange(BCH)
    table = np.zeros((BCH, 2, 8, 2, BCH), np.float32)
    for v in range(2):
        table[i, v, :, v, i] = 1.0
    return table.reshape(16 * BCH, 2 * BCH).astype(ml_dtypes.bfloat16)


def spectra_kernel(members, groups, meta, x_ref, table_ref, *rest):
    own_refs = rest[:members]
    send_refs = rest[members : members + CHUNKS]
    held, own_sem, send_sem = rest[members + CHUNKS :]
    step = pl.program_id(0)
    polarity = 1.0 - 2.0 * meta[2 * groups + step].astype(jnp.float32)
    for w in range(2):
        spectra = lax.dot_general(
            table_ref[...],
            x_ref[:, w * WS : (w + 1) * WS],
            (((1,), (1,)), ((), ())),
            preferred_element_type=jnp.float32,
        )
        power = jnp.sum(spectra * spectra, axis=0, keepdims=True) / BINS
        white = spectra * (polarity / jnp.sqrt(power + 1e-06))
        for o in range(OCT):
            tile = jnp.concatenate(
                [white[o * 8 : o * 8 + 8], white[BINS + o * 8 : BINS + o * 8 + 8]], 0
            )
            held[step, o * 32 + w * 16 : o * 32 + w * 16 + 16, :] = tile.astype(jnp.bfloat16)

    @pl.when(step == members - 1)
    def _():
        copies = []
        me = meta[2 * groups + members]
        for k in range(members):
            src = held.at[lax.rem(me + k, members)]
            copies.append(pltpu.make_async_copy(src, own_refs[k], own_sem.at[k]))
        rows = ROWS // CHUNKS
        for c in range(CHUNKS):
            for j in range(2 * groups):
                src = held.at[meta[j], pl.ds(c * rows, rows), :]
                copies.append(
                    pltpu.make_async_copy(src, send_refs[c].at[j], send_sem.at[c, j])
                )
        for copy in copies:
            copy.start()
        for copy in copies:
            copy.wait()


def pack_kernel(members, pairs, meta, in_ref, *rest):
    out_refs, sem = rest[:members], rest[members]
    me = meta[members * pairs]
    copies = []
    for k in range(members):
        target = lax.rem(me + k, members)
        for q in range(pairs):
            src = in_ref.at[meta[target * pairs + q]]
            copies.append(
                pltpu.make_async_copy(src, out_refs[k].at[q], sem.at[k * pairs + q])
            )
    for copy in copies:
        copy.start()
    for copy in copies:
        copy.wait()


def pair_kernel(members, pairs, spread_ref, lag_ref, *rest):
    own_refs = rest[:members]
    part_refs = rest[members : 2 * members]
    out_ref = rest[2 * members]
    cross_ref = rest[2 * members + 1]
    step = pl.program_id(0)
    depth = members * 32

    @pl.when(step < OCT)
    def _():
        rows = pl.ds(pl.multiple_of(step * 32, 32), 32)
        own = jnp.concatenate([r[rows, :] for r in own_refs], 0)
        halves = own.astype(jnp.float32).reshape(depth // 16, 2, 8, BCH)
        turned = jnp.stack([halves[:, 1], -halves[:, 0]], axis=1)
        turned = turned.reshape(depth, BCH).astype(jnp.bfloat16)
        both = jnp.concatenate([own, turned], 1)
        right = jnp.concatenate(
            [jnp.concatenate([r[q, rows, :] for r in part_refs], 0) for q in range(pairs)], 1
        )
        same = (
            lax.broadcasted_iota(jnp.int32, (256, depth), 0) % 8
            == lax.broadcasted_iota(jnp.int32, (256, depth), 1) % 8
        )

        def body(ib, _):
            at = pl.ds(pl.multiple_of(ib * 256, 256), 256)
            left = lax.dot_general(
                spread_ref[at, :],
                both,
                (((1,), (1,)), ((), ())),
                preferred_element_type=jnp.float32,
            )
            left = jnp.where(same, left, 0.0).astype(jnp.bfloat16)
            cross = jnp.dot(left, right, preferred_element_type=jnp.float32)
            cross_ref[step, pl.ds(ib * 16, 16)] = cross.astype(jnp.bfloat16).reshape(
                16, 16, pairs * BCH
            )
            return 0

        lax.fori_loop(0, BCH // 16, body, 0)

    @pl.when(step >= OCT)
    def _():
        scale = 1.0 / math.sqrt(members * 2 * BINS)
        for ii in range(8):
            i = (step - OCT) * 8 + ii
            right = cross_ref[:, i].reshape(2 * BINS, pairs * BCH)
            lagged = jnp.dot(lag_ref[...], right, preferred_element_type=jnp.float32)
            lagged = (lagged * scale).astype(jnp.bfloat16)
            for q in range(pairs):
                out_ref[q, :, ii * BCH : (ii + 1) * BCH] = lagged[:, q * BCH : (q + 1) * BCH]


def shards(record, deck_ids, partners):
    groups = lax.axis_size("blk")
    members = lax.axis_size("win")
    group = lax.axis_index("blk")
    member = lax.axis_index("win")
    pairs = partners.shape[1]
    any_space = pl.BlockSpec(memory_space=pl.ANY)

    listed = partners.reshape(groups, members * pairs)
    here = listed // members == group
    first = jnp.min(jnp.where(here, listed % members, members), axis=1)
    second = jnp.max(jnp.where(here, listed % members, -1), axis=1)
    slots = jnp.stack([first, second], axis=1).reshape(-1)
    decks = lax.dynamic_slice_in_dim(deck_ids, group * members, members, 0)
    meta = jnp.concatenate([slots, decks, member.reshape(1)]).astype(jnp.int32)
    wanted = lax.dynamic_slice_in_dim(listed, group, 1, 0).reshape(-1)
    lower = (wanted[None, :] // members == wanted[:, None] // members) & (
        wanted[None, :] < wanted[:, None]
    )
    place = 2 * (wanted // members) + jnp.any(lower, axis=1).astype(jnp.int32)
    place = jnp.concatenate([place, member.reshape(1)]).astype(jnp.int32)

    rows = ROWS // CHUNKS
    outs = pl.pallas_call(
        functools.partial(spectra_kernel, members, groups),
        grid_spec=pltpu.PrefetchScalarGridSpec(
            num_scalar_prefetch=1,
            grid=(members,),
            in_specs=[
                pl.BlockSpec((BCH, 2 * WS), lambda b, meta: (b, 0)),
                pl.BlockSpec((2 * BINS, WS), lambda b, meta: (0, 0)),
            ],
            out_specs=[any_space] * (members + CHUNKS),
            scratch_shapes=[
                pltpu.VMEM((members, ROWS, BCH), jnp.bfloat16),
                pltpu.SemaphoreType.DMA((members,)),
                pltpu.SemaphoreType.DMA((CHUNKS, 2 * groups)),
            ],
        ),
        out_shape=[jax.ShapeDtypeStruct((ROWS, BCH), jnp.bfloat16)] * members
        + [jax.ShapeDtypeStruct((2 * groups, rows, BCH), jnp.bfloat16)] * CHUNKS,
        compiler_params=pltpu.CompilerParams(vmem_limit_bytes=VMEM_LIMIT),
        name="spectra",
    )(meta, record, jnp.asarray(forward_table()))
    own, sends = list(outs[:members]), outs[members:]

    def shift(k):
        return [(m, (m + k) % members) for m in range(members)]

    own = [own[0]] + [lax.ppermute(own[k], "win", shift(k)) for k in range(1, members)]
    got = lax.all_to_all(
        sends[0].reshape(groups, 2 * rows, BCH), "blk", split_axis=0, concat_axis=0, tiled=True
    )
    parts = pl.pallas_call(
        functools.partial(pack_kernel, members, pairs),
        grid_spec=pltpu.PrefetchScalarGridSpec(
            num_scalar_prefetch=1,
            grid=(),
            in_specs=[any_space],
            out_specs=[any_space] * members,
            scratch_shapes=[pltpu.SemaphoreType.DMA((members * pairs,))],
        ),
        out_shape=[jax.ShapeDtypeStruct((pairs, rows, BCH), jnp.bfloat16)] * members,
        name="pack",
    )(place, got.reshape(2 * groups, rows, BCH))
    parts = [parts[0]] + [lax.ppermute(parts[k], "win", shift(k)) for k in range(1, members)]

    def whole(shape):
        return pl.BlockSpec(shape, lambda s: (0,) * len(shape))

    return pl.pallas_call(
        functools.partial(pair_kernel, members, pairs),
        grid=(2 * OCT,),
        in_specs=[whole((16 * BCH, 2 * BCH)), whole((LAGS, 2 * BINS))]
        + [whole((ROWS, BCH))] * members
        + [whole((pairs, rows, BCH))] * members,
        out_specs=pl.BlockSpec(
            (pairs, LAGS, 8 * BCH), lambda s: (0, 0, jnp.maximum(s - OCT, 0))
        ),
        out_shape=jax.ShapeDtypeStruct((pairs, LAGS, BCH * BCH), jnp.bfloat16),
        scratch_shapes=[pltpu.VMEM((OCT, BCH, 16, pairs * BCH), jnp.bfloat16)],
        compiler_params=pltpu.CompilerParams(vmem_limit_bytes=VMEM_LIMIT),
        name="correlate",
    )(jnp.asarray(spread_table()), jnp.asarray(lag_table()), *own, *parts)


def solution(mesh):
    return jax.shard_map(
        shards,
        mesh=mesh,
        in_specs=(P("blk", "win"), P(), P()),
        out_specs=P(("blk", "win"), None, None),
        check_vma=False,
    )
```

```python
import functools
import math

import jax
import jax.numpy as jnp
import ml_dtypes
import numpy as np
from jax import lax
from jax.experimental import pallas as pl
from jax.experimental.pallas import tpu as pltpu
from jax.sharding import PartitionSpec as P

WS = 512
BINS = 128
LAGS = 64
BCH = 128
OCT = BINS // 8
ROWS = OCT * 32
CHUNKS = 2
VMEM_LIMIT = 56 * 1024 * 1024


def forward_table():
    t = np.arange(WS)
    f = np.arange(1, BINS + 1)
    angle = (f[:, None] * t[None, :] % WS) * (2.0 * math.pi / WS)
    return np.concatenate([np.cos(angle), -np.sin(angle)], 0).astype(ml_dtypes.bfloat16)


def lag_table():
    f = np.arange(1, BINS + 1)
    s = np.arange(LAGS) - LAGS // 2
    angle = (s[:, None] * f[None, :] % WS) * (2.0 * math.pi / WS)
    both = np.stack([np.cos(angle), -np.sin(angle)], 1).reshape(LAGS, 2, OCT, 8)
    return both.transpose(0, 2, 1, 3).reshape(LAGS, 2 * BINS).astype(ml_dtypes.bfloat16)


def spread_table():
    i = np.arange(BCH)
    table = np.zeros((BCH, 2, 8, 2, BCH), np.float32)
    for v in range(2):
        table[i, v, :, v, i] = 1.0
    return table.reshape(16 * BCH, 2 * BCH).astype(ml_dtypes.bfloat16)


def spectra_kernel(members, groups, meta, x_ref, table_ref, *rest):
    own_refs = rest[:members]
    send_refs = rest[members : members + CHUNKS]
    held, own_sem, send_sem = rest[members + CHUNKS :]
    step = pl.program_id(0)
    polarity = 1.0 - 2.0 * meta[2 * groups + step].astype(jnp.float32)
    for w in range(2):
        spectra = lax.dot_general(
            table_ref[...],
            x_ref[:, w * WS : (w + 1) * WS],
            (((1,), (1,)), ((), ())),
            preferred_element_type=jnp.float32,
        )
        power = jnp.sum(spectra * spectra, axis=0, keepdims=True) / BINS
        white = spectra * (polarity / jnp.sqrt(power + 1e-06))
        for o in range(OCT):
            tile = jnp.concatenate(
                [white[o * 8 : o * 8 + 8], white[BINS + o * 8 : BINS + o * 8 + 8]], 0
            )
            held[step, o * 32 + w * 16 : o * 32 + w * 16 + 16, :] = tile.astype(jnp.bfloat16)

    @pl.when(step == members - 1)
    def _():
        copies = []
        me = meta[2 * groups + members]
        for k in range(members):
            src = held.at[lax.rem(me + k, members)]
            copies.append(pltpu.make_async_copy(src, own_refs[k], own_sem.at[k]))
        rows = ROWS // CHUNKS
        for c in range(CHUNKS):
            for j in range(2 * groups):
                src = held.at[meta[j], pl.ds(c * rows, rows), :]
                copies.append(
                    pltpu.make_async_copy(src, send_refs[c].at[j], send_sem.at[c, j])
                )
        for copy in copies:
            copy.start()
        for copy in copies:
            copy.wait()


def pack_kernel(members, pairs, meta, in_ref, *out_refs):
    me = meta[members * pairs]
    for k in range(members):
        target = lax.rem(me + k, members)
        for q in range(pairs):
            out_refs[k][q] = in_ref[meta[target * pairs + q]]


def left_kernel(members, spread_ref, *rest):
    own_refs, left_ref = rest[:members], rest[members]
    depth = members * 32
    rows = pl.ds(pl.multiple_of(pl.program_id(0) * 32, 32), 32)
    own = jnp.concatenate([r[rows, :] for r in own_refs], 0)
    halves = own.astype(jnp.float32).reshape(depth // 16, 2, 8, BCH)
    turned = jnp.stack([halves[:, 1], -halves[:, 0]], axis=1)
    turned = turned.reshape(depth, BCH).astype(jnp.bfloat16)
    both = jnp.concatenate([own, turned], 1)
    same = (
        lax.broadcasted_iota(jnp.int32, (256, depth), 0) % 8
        == lax.broadcasted_iota(jnp.int32, (256, depth), 1) % 8
    )
    for ib in range(BCH // 16):
        at = slice(ib * 256, (ib + 1) * 256)
        left = lax.dot_general(
            spread_ref[at, :],
            both,
            (((1,), (1,)), ((), ())),
            preferred_element_type=jnp.float32,
        )
        left_ref[0, at, :] = jnp.where(same, left, 0.0).astype(jnp.bfloat16)


def cross_octet(members, pairs, octet, left_ref, part_refs):
    rows = pl.ds(pl.multiple_of(octet * 32, 32), 32)
    right = jnp.concatenate(
        [jnp.concatenate([r[q, rows, :] for r in part_refs], 0) for q in range(pairs)], 1
    )
    for ib in range(BCH // 16):
        left = left_ref[0, ib * 256 : (ib + 1) * 256, :]
        cross = jnp.dot(left, right, preferred_element_type=jnp.float32)
        yield ib * 16, cross.astype(jnp.bfloat16).reshape(16, 16, pairs * BCH)


def cross_kernel(members, pairs, left_ref, *rest):
    part_refs, cross_ref = rest[:members], rest[members]
    for i, cross in cross_octet(members, pairs, pl.program_id(0), left_ref, part_refs):
        cross_ref[0, i : i + 16] = cross


def pair_kernel(members, pairs, octets, left_ref, lag_ref, *rest):
    part_refs = rest[:members]
    early_refs = rest[members : members + CHUNKS - 1]
    out_ref = rest[members + CHUNKS - 1]
    last_ref = rest[members + CHUNKS]
    step = pl.program_id(0)

    @pl.when(step < octets)
    def _():
        for i, cross in cross_octet(members, pairs, step, left_ref, part_refs):
            last_ref[step, i : i + 16] = cross

    @pl.when(step >= octets)
    def _():
        scale = 1.0 / math.sqrt(members * 2 * BINS)
        for ii in range(8):
            i = (step - octets) * 8 + ii
            right = jnp.concatenate([r[:, ii] for r in early_refs] + [last_ref[:, i]], 0)
            right = right.reshape(2 * BINS, pairs * BCH)
            lagged = jnp.dot(lag_ref[...], right, preferred_element_type=jnp.float32)
            lagged = (lagged * scale).astype(jnp.bfloat16)
            for q in range(pairs):
                out_ref[q, :, ii * BCH : (ii + 1) * BCH] = lagged[:, q * BCH : (q + 1) * BCH]


def shards(record, deck_ids, partners):
    groups = lax.axis_size("blk")
    members = lax.axis_size("win")
    group = lax.axis_index("blk")
    member = lax.axis_index("win")
    pairs = partners.shape[1]
    any_space = pl.BlockSpec(memory_space=pl.ANY)

    def whole(shape):
        return pl.BlockSpec(shape, lambda *_: (0,) * len(shape))

    def shift(k):
        return [(m, (m + k) % members) for m in range(members)]

    listed = partners.reshape(groups, members * pairs)
    here = listed // members == group
    first = jnp.min(jnp.where(here, listed % members, members), axis=1)
    second = jnp.max(jnp.where(here, listed % members, -1), axis=1)
    slots = jnp.stack([first, second], axis=1).reshape(-1)
    decks = lax.dynamic_slice_in_dim(deck_ids, group * members, members, 0)
    meta = jnp.concatenate([slots, decks, member.reshape(1)]).astype(jnp.int32)
    wanted = lax.dynamic_slice_in_dim(listed, group, 1, 0).reshape(-1)
    lower = (wanted[None, :] // members == wanted[:, None] // members) & (
        wanted[None, :] < wanted[:, None]
    )
    place = 2 * (wanted // members) + jnp.any(lower, axis=1).astype(jnp.int32)
    place = jnp.concatenate([place, member.reshape(1)]).astype(jnp.int32)

    rows = ROWS // CHUNKS
    outs = pl.pallas_call(
        functools.partial(spectra_kernel, members, groups),
        grid_spec=pltpu.PrefetchScalarGridSpec(
            num_scalar_prefetch=1,
            grid=(members,),
            in_specs=[
                pl.BlockSpec((BCH, 2 * WS), lambda b, meta: (b, 0)),
                pl.BlockSpec((2 * BINS, WS), lambda b, meta: (0, 0)),
            ],
            out_specs=[any_space] * (members + CHUNKS),
            scratch_shapes=[
                pltpu.VMEM((members, ROWS, BCH), jnp.bfloat16),
                pltpu.SemaphoreType.DMA((members,)),
                pltpu.SemaphoreType.DMA((CHUNKS, 2 * groups)),
            ],
        ),
        out_shape=[jax.ShapeDtypeStruct((ROWS, BCH), jnp.bfloat16)] * members
        + [jax.ShapeDtypeStruct((2 * groups, rows, BCH), jnp.bfloat16)] * CHUNKS,
        compiler_params=pltpu.CompilerParams(vmem_limit_bytes=VMEM_LIMIT),
        name="spectra",
    )(meta, record, jnp.asarray(forward_table()))
    own, sends = list(outs[:members]), list(outs[members:])

    own = [own[0]] + [lax.ppermute(own[k], "win", shift(k)) for k in range(1, members)]
    octets = OCT // CHUNKS
    left = pl.pallas_call(
        functools.partial(left_kernel, members),
        grid=(OCT,),
        in_specs=[whole((16 * BCH, 2 * BCH))] + [whole((ROWS, BCH))] * members,
        out_specs=pl.BlockSpec((1, 16 * BCH, 32 * members), lambda s: (s, 0, 0)),
        out_shape=jax.ShapeDtypeStruct((OCT, 16 * BCH, 32 * members), jnp.bfloat16),
        compiler_params=pltpu.CompilerParams(vmem_limit_bytes=VMEM_LIMIT),
        cost_estimate=pl.CostEstimate(
            flops=10_000_000_000, bytes_accessed=2**24, transcendentals=0
        ),
        name="left",
    )(jnp.asarray(spread_table()), *own)

    def exchange(send):
        return lax.all_to_all(
            send.reshape(groups, 2 * rows, BCH), "blk", split_axis=0, concat_axis=0, tiled=True
        )

    def deliver(got):
        parts = pl.pallas_call(
            functools.partial(pack_kernel, members, pairs),
            grid_spec=pltpu.PrefetchScalarGridSpec(
                num_scalar_prefetch=1,
                grid=(1,),
                in_specs=[whole((2 * groups, rows, BCH))],
                out_specs=[whole((pairs, rows, BCH))] * members,
            ),
            out_shape=[jax.ShapeDtypeStruct((pairs, rows, BCH), jnp.bfloat16)] * members,
            compiler_params=pltpu.CompilerParams(vmem_limit_bytes=VMEM_LIMIT),
            name="pack",
        )(place, got.reshape(2 * groups, rows, BCH))
        return [parts[0]] + [lax.ppermute(parts[k], "win", shift(k)) for k in range(1, members)]

    def crossed(c, parts):
        return pl.pallas_call(
            functools.partial(cross_kernel, members, pairs),
            grid=(octets,),
            in_specs=[
                pl.BlockSpec(
                    (1, 16 * BCH, 32 * members), lambda s: (c * octets + s, 0, 0)
                )
            ]
            + [whole((pairs, rows, BCH))] * members,
            out_specs=pl.BlockSpec((1, BCH, 16, pairs * BCH), lambda s: (s, 0, 0, 0)),
            out_shape=jax.ShapeDtypeStruct((octets, BCH, 16, pairs * BCH), jnp.bfloat16),
            compiler_params=pltpu.CompilerParams(vmem_limit_bytes=VMEM_LIMIT),
            cost_estimate=pl.CostEstimate(
                flops=20_000_000_000 // CHUNKS, bytes_accessed=2**25, transcendentals=0
            ),
            name="cross",
        )(left, *parts)

    early = []
    for c in range(CHUNKS):
        got = exchange(sends[c])
        if c == 0:
            got, left = lax.optimization_barrier((got, left))
        else:
            got, parts = lax.optimization_barrier((got, parts))
        if c < CHUNKS - 1:
            got, sends[c + 1] = lax.optimization_barrier((got, sends[c + 1]))
        if c > 0:
            early.append(crossed(c - 1, parts))
        parts = deliver(got)

    def after(s):
        return jnp.maximum(s - octets, 0)

    return pl.pallas_call(
        functools.partial(pair_kernel, members, pairs, octets),
        grid=(octets + OCT,),
        in_specs=[
            pl.BlockSpec(
                (1, 16 * BCH, 32 * members),
                lambda s: (jnp.minimum(OCT - octets + s, OCT - 1), 0, 0),
            ),
            whole((LAGS, 2 * BINS)),
        ]
        + [whole((pairs, rows, BCH))] * members
        + [pl.BlockSpec((octets, 8, 16, pairs * BCH), lambda s: (0, after(s), 0, 0))]
        * (CHUNKS - 1),
        out_specs=pl.BlockSpec((pairs, LAGS, 8 * BCH), lambda s: (0, 0, after(s))),
        out_shape=jax.ShapeDtypeStruct((pairs, LAGS, BCH * BCH), jnp.bfloat16),
        scratch_shapes=[pltpu.VMEM((octets, BCH, 16, pairs * BCH), jnp.bfloat16)],
        compiler_params=pltpu.CompilerParams(vmem_limit_bytes=VMEM_LIMIT),
        name="correlate",
    )(left, jnp.asarray(lag_table()), *parts, *early)


def solution(mesh):
    return jax.shard_map(
        shards,
        mesh=mesh,
        in_specs=(P("blk", "win"), P(), P()),
        out_specs=P(("blk", "win"), None, None),
        check_vma=False,
    )
```

```python
import functools
import math

import jax
import jax.numpy as jnp
import ml_dtypes
import numpy as np
from jax import lax
from jax.experimental import pallas as pl
from jax.experimental.pallas import tpu as pltpu
from jax.sharding import PartitionSpec as P

WS = 512
BINS = 128
LAGS = 64
BCH = 128
OCT = BINS // 8
ROWS = OCT * 32
SPLIT = (5, 5, 4, 2)
BEGIN = tuple(sum(SPLIT[:c]) for c in range(len(SPLIT)))
LAST = len(SPLIT) - 1
HOPS = ((0, 0), (1, 0), (3, 0), (1, 1), (3, 1), (2, 0), (2, 1), (0, 1))
VMEM_LIMIT = 56 * 1024 * 1024
PARAMS = pltpu.CompilerParams(vmem_limit_bytes=VMEM_LIMIT)


def forward_table():
    t = np.arange(WS)
    f = np.arange(1, BINS + 1)
    angle = (f[:, None] * t[None, :] % WS) * (2.0 * math.pi / WS)
    return np.concatenate([np.cos(angle), -np.sin(angle)], 0).astype(ml_dtypes.bfloat16)


def lag_table():
    f = np.arange(1, BINS + 1)
    s = np.arange(LAGS) - LAGS // 2
    angle = (s[:, None] * f[None, :] % WS) * (2.0 * math.pi / WS)
    both = np.stack([np.cos(angle), -np.sin(angle)], 1).reshape(LAGS, 2, OCT, 8)
    return both.transpose(0, 2, 1, 3).reshape(LAGS, 2 * BINS).astype(ml_dtypes.bfloat16)


def target(me, hop, members):
    z = lax.rem(me // 2 + hop[0], members // 2)
    return 2 * z + lax.rem(me + hop[1], 2)


def spectra_kernel(members, groups, meta, x_ref, table_ref, white_ref, send_ref, *own_refs):
    step = pl.program_id(0)
    polarity = 1.0 - 2.0 * meta[2 * groups + step].astype(jnp.float32)
    for w in range(2):
        spectra = lax.dot_general(
            table_ref[...],
            x_ref[:, w * WS : (w + 1) * WS],
            (((1,), (1,)), ((), ())),
            preferred_element_type=jnp.float32,
        )
        power = jnp.sum(spectra * spectra, axis=0, keepdims=True) / BINS
        white = spectra * (polarity / jnp.sqrt(power + 1e-06))
        for o in range(OCT):
            tile = jnp.concatenate(
                [white[o * 8 : o * 8 + 8], white[BINS + o * 8 : BINS + o * 8 + 8]], 0
            )
            white_ref[step, o * 32 + w * 16 : o * 32 + w * 16 + 16, :] = tile.astype(jnp.bfloat16)

    @pl.when(step == members - 1)
    def _():
        me = meta[2 * groups + members]
        for j in range(2 * groups):
            send_ref[j] = white_ref[meta[j], : 32 * SPLIT[0], :]
        for hop, own_ref in zip(HOPS, own_refs, strict=True):
            own_ref[...] = white_ref[target(me, hop, members)]


def send_kernel(meta, white_ref, *send_refs):
    for c, send_ref in enumerate(send_refs, 1):
        for j in range(send_ref.shape[0]):
            send_ref[j] = white_ref[meta[j], pl.ds(32 * BEGIN[c], 32 * SPLIT[c]), :]


def pack_kernel(members, pairs, meta, in_ref, *out_refs):
    me = meta[members * pairs]
    for hop, out_ref in zip(HOPS, out_refs, strict=True):
        to = target(me, hop, members)
        for q in range(pairs):
            out_ref[q] = in_ref[meta[to * pairs + q]]


def cross_octet(octet, local, own_refs, part_refs, rows_ref, store):
    pairs = part_refs[0].shape[0]
    depth = 32 * len(own_refs)
    at = pl.ds(pl.multiple_of(octet * 32, 32), 32)
    own = jnp.concatenate([r[at, :] for r in own_refs], 0).astype(jnp.float32)
    halves = own.reshape(depth // 16, 2, 8, BCH)
    turned = jnp.stack([halves[:, 1], -halves[:, 0]], axis=1).reshape(depth, BCH)
    rows_ref[0] = own.T
    rows_ref[1] = turned.T
    at = pl.ds(pl.multiple_of(local * 32, 32), 32)
    right = jnp.concatenate(
        [jnp.concatenate([r[q, at, :] for r in part_refs], 0) for q in range(pairs)], 1
    )
    same = (
        lax.broadcasted_iota(jnp.int32, (8, depth), 0)
        == lax.broadcasted_iota(jnp.int32, (8, depth), 1) % 8
    )
    for i0 in range(0, BCH, 16):
        tiles = []
        for i in range(i0, i0 + 16):
            for v in range(2):
                row = rows_ref[v, pl.ds(i, 8, stride=0), :]
                tiles.append(jnp.where(same, row, 0.0))
        left = jnp.concatenate(tiles, 0).astype(jnp.bfloat16)
        cross = jnp.dot(left, right, preferred_element_type=jnp.float32)
        store(i0, cross.astype(jnp.bfloat16).reshape(16, 16, pairs * BCH))


def cross_kernel(members, begin, *refs):
    own_refs, part_refs = refs[:members], refs[members : 2 * members]
    cross_ref, rows_ref = refs[2 * members :]
    step = pl.program_id(0)

    def store(i0, value):
        cross_ref[0, i0 : i0 + 16] = value

    cross_octet(begin + step, step, own_refs, part_refs, rows_ref, store)


def pair_kernel(members, lag_ref, *refs):
    own_refs, part_refs = refs[:members], refs[members : 2 * members]
    early_refs = refs[2 * members : 2 * members + LAST]
    out_ref, cross_ref, rows_ref, sem = refs[2 * members + LAST :]
    pairs = out_ref.shape[0]
    octets = SPLIT[LAST]
    step = pl.program_id(0)

    def fetch(c, block):
        at = pl.ds(block * 8, 8)
        return pltpu.make_async_copy(
            early_refs[c].at[:, at],
            cross_ref.at[pl.ds(BEGIN[c], SPLIT[c]), at],
            sem.at[c, block],
        )

    @pl.when(step == 0)
    def _():
        for block in range(BCH // 8):
            for c in range(LAST):
                fetch(c, block).start()

    @pl.when(step < octets)
    def _():
        def store(i0, value):
            cross_ref[BEGIN[LAST] + step, i0 : i0 + 16] = value

        cross_octet(BEGIN[LAST] + step, step, own_refs, part_refs, rows_ref, store)

    @pl.when(step >= octets)
    def _():
        block = step - octets
        for c in range(LAST):
            fetch(c, block).wait()
        scale = 1.0 / math.sqrt(members * 2 * BINS)
        for ii in range(8):
            right = cross_ref[:, block * 8 + ii].reshape(2 * BINS, pairs * BCH)
            lagged = jnp.dot(lag_ref[...], right, preferred_element_type=jnp.float32)
            lagged = (lagged * scale).astype(jnp.bfloat16)
            for q in range(pairs):
                out_ref[q, :, ii * BCH : (ii + 1) * BCH] = lagged[:, q * BCH : (q + 1) * BCH]


def whole(shape):
    return pl.BlockSpec(shape, lambda *_: (0,) * len(shape))


def bf16(*shape):
    return jax.ShapeDtypeStruct(shape, jnp.bfloat16)


def prefetched(grid, in_shapes, out_shapes):
    return pltpu.PrefetchScalarGridSpec(
        num_scalar_prefetch=1,
        grid=grid,
        in_specs=[whole(s) for s in in_shapes],
        out_specs=[whole(s) for s in out_shapes],
    )


def correlate(own, parts, early, pairs):
    members = len(own)
    octets = SPLIT[LAST]

    def after(s):
        return jnp.maximum(s - octets, 0)

    return pl.pallas_call(
        functools.partial(pair_kernel, members),
        grid=(octets + BCH // 8,),
        in_specs=[whole((LAGS, 2 * BINS))]
        + [whole(x.shape) for x in (*own, *parts)]
        + [pl.BlockSpec(memory_space=pl.ANY)] * LAST,
        out_specs=pl.BlockSpec((pairs, LAGS, 8 * BCH), lambda s: (0, 0, after(s))),
        out_shape=bf16(pairs, LAGS, BCH * BCH),
        scratch_shapes=[
            pltpu.VMEM((OCT, BCH, 16, pairs * BCH), jnp.bfloat16),
            pltpu.VMEM((2, BCH, 32 * members), jnp.float32),
            pltpu.SemaphoreType.DMA((LAST, BCH // 8)),
        ],
        compiler_params=PARAMS,
        name="correlate",
    )(jnp.asarray(lag_table()), *own, *parts, *early)


def crossed(c, own, parts, pairs):
    members = len(own)
    return pl.pallas_call(
        functools.partial(cross_kernel, members, BEGIN[c]),
        grid=(SPLIT[c],),
        in_specs=[whole(x.shape) for x in (*own, *parts)],
        out_specs=pl.BlockSpec((1, BCH, 16, pairs * BCH), lambda s: (s, 0, 0, 0)),
        out_shape=bf16(SPLIT[c], BCH, 16, pairs * BCH),
        scratch_shapes=[pltpu.VMEM((2, BCH, 32 * members), jnp.float32)],
        compiler_params=PARAMS,
        cost_estimate=pl.CostEstimate(
            flops=2_000_000_000 * SPLIT[c], bytes_accessed=2**21 * SPLIT[c], transcendentals=0
        ),
        name="cross",
    )(*own, *parts)


def shards(record, deck_ids, partners):
    groups = lax.axis_size("blk")
    members = lax.axis_size("win")
    group = lax.axis_index("blk")
    member = lax.axis_index("win")
    pairs = partners.shape[1]

    def move(pieces):
        moved = [pieces[0]]
        for (dz, dc), piece in zip(HOPS[1:], pieces[1:], strict=True):
            ring = members // 2
            way = [(m, (m // 2 + dz) % ring * 2 + (m + dc) % 2) for m in range(members)]
            moved.append(lax.ppermute(piece, "win", way))
        return moved

    listed = partners.reshape(groups, members * pairs)
    here = listed // members == group
    first = jnp.min(jnp.where(here, listed % members, members), axis=1)
    second = jnp.max(jnp.where(here, listed % members, -1), axis=1)
    slots = jnp.stack([first, second], axis=1).reshape(-1)
    decks = lax.dynamic_slice_in_dim(deck_ids, group * members, members, 0)
    meta = jnp.concatenate([slots, decks, member.reshape(1)]).astype(jnp.int32)
    wanted = lax.dynamic_slice_in_dim(listed, group, 1, 0).reshape(-1)
    lower = (wanted[None, :] // members == wanted[:, None] // members) & (
        wanted[None, :] < wanted[:, None]
    )
    place = 2 * (wanted // members) + jnp.any(lower, axis=1).astype(jnp.int32)
    place = jnp.concatenate([place, member.reshape(1)]).astype(jnp.int32)

    white_shape = (members, ROWS, BCH)
    send_shapes = [(2 * groups, 32 * n, BCH) for n in SPLIT]
    shapes = [white_shape, send_shapes[0]] + [(ROWS, BCH)] * members
    white, send, *own = pl.pallas_call(
        functools.partial(spectra_kernel, members, groups),
        grid_spec=pltpu.PrefetchScalarGridSpec(
            num_scalar_prefetch=1,
            grid=(members,),
            in_specs=[
                pl.BlockSpec((BCH, 2 * WS), lambda b, meta: (b, 0)),
                whole((2 * BINS, WS)),
            ],
            out_specs=[whole(s) for s in shapes],
        ),
        out_shape=[bf16(*s) for s in shapes],
        compiler_params=PARAMS,
        name="spectra",
    )(meta, record, jnp.asarray(forward_table()))
    sends = pl.pallas_call(
        send_kernel,
        grid_spec=prefetched((1,), [white_shape], send_shapes[1:]),
        out_shape=[bf16(*s) for s in send_shapes[1:]],
        compiler_params=PARAMS,
        cost_estimate=pl.CostEstimate(flops=0, bytes_accessed=2**23, transcendentals=0),
        name="send",
    )(meta, white)
    sends = [send, *sends]
    own = move(own)

    early = []
    parts = None
    for c, octets in enumerate(SPLIT):
        got = lax.all_to_all(
            sends[c].reshape(groups, 64 * octets, BCH),
            "blk",
            split_axis=0,
            concat_axis=0,
            tiled=True,
        )
        if c == 0:
            got, own, place = lax.optimization_barrier((got, own, place))
        else:
            got, parts = lax.optimization_barrier((got, parts))
            early.append(crossed(c - 1, own, parts, pairs))
        if c >= 2:
            got, early[c - 2] = lax.optimization_barrier((got, early[c - 2]))
        if c < LAST:
            got, sends[c + 1] = lax.optimization_barrier((got, sends[c + 1]))
        parts = pl.pallas_call(
            functools.partial(pack_kernel, members, pairs),
            grid_spec=prefetched(
                (1,), [send_shapes[c]], [(pairs, 32 * octets, BCH)] * members
            ),
            out_shape=[bf16(pairs, 32 * octets, BCH)] * members,
            compiler_params=PARAMS,
            name="pack",
        )(place, got.reshape(send_shapes[c]))
        parts = move(parts)
    return correlate(own, parts, early, pairs)


def solution(mesh):
    return jax.shard_map(
        shards,
        mesh=mesh,
        in_specs=(P("blk", "win"), P(), P()),
        out_specs=P(("blk", "win"), None, None),
        check_vma=False,
    )
```

```python
import functools
import math

import jax
import jax.numpy as jnp
import ml_dtypes
import numpy as np
from jax import lax
from jax.experimental import pallas as pl
from jax.experimental.pallas import tpu as pltpu
from jax.sharding import PartitionSpec as P

WS = 512
BINS = 128
LAGS = 64
BCH = 128
OCT = BINS // 8
ROWS = OCT * 32
SPLIT = (7, 9)
BEGIN = tuple(sum(SPLIT[:c]) for c in range(len(SPLIT)))
LAST = len(SPLIT) - 1
AT_ONCE = 4
HOPS = ((0, 0), (1, 0), (3, 0), (1, 1), (3, 1), (2, 0), (2, 1), (0, 1))
IN_VMEM = pl.BlockSpec(memory_space=pltpu.VMEM)


def forward_table():
    t = np.arange(WS)
    f = np.arange(1, BINS + 1)
    angle = (f[:, None] * t[None, :] % WS) * (2.0 * math.pi / WS)
    return np.concatenate([np.cos(angle), -np.sin(angle)], 0).astype(ml_dtypes.bfloat16)


def lag_table():
    f = np.arange(1, BINS + 1)
    s = np.arange(LAGS) - LAGS // 2
    angle = (s[:, None] * f[None, :] % WS) * (2.0 * math.pi / WS)
    both = np.stack([np.cos(angle), -np.sin(angle)], 1).reshape(LAGS, 2, OCT, 8)
    return both.transpose(0, 2, 1, 3).reshape(LAGS, 2 * BINS).astype(ml_dtypes.bfloat16)


def target(me, hop, members):
    z = lax.rem(me // 2 + hop[0], members // 2)
    return 2 * z + lax.rem(me + hop[1], 2)


def spectra_kernel(members, groups, meta, x_ref, table_ref, white_ref, send_ref, *own_refs):
    step = pl.program_id(0)
    for w in range(2):
        spectra = lax.dot_general(
            table_ref[...],
            x_ref[:, w * WS : (w + 1) * WS],
            (((1,), (1,)), ((), ())),
            preferred_element_type=jnp.float32,
        )
        power = jnp.sum(spectra * spectra, axis=0, keepdims=True) / BINS
        root = jnp.sqrt(power + 1e-06)
        for b in range(AT_ONCE):
            block = step * AT_ONCE + b
            at = slice(b * BCH, (b + 1) * BCH)
            polarity = 1.0 - 2.0 * meta[2 * groups + block].astype(jnp.float32)
            white = spectra[:, at] * (polarity / root[:, at])
            for o in range(OCT):
                tile = jnp.concatenate(
                    [white[o * 8 : o * 8 + 8], white[BINS + o * 8 : BINS + o * 8 + 8]], 0
                )
                row = o * 32 + w * 16
                white_ref[block, row : row + 16, :] = tile.astype(jnp.bfloat16)

    @pl.when(step == members // AT_ONCE - 1)
    def _():
        me = meta[2 * groups + members]
        for j in range(2 * groups):
            send_ref[j] = white_ref[meta[j], : 32 * SPLIT[0], :]
        for hop, own_ref in zip(HOPS, own_refs, strict=True):
            own_ref[...] = white_ref[target(me, hop, members)]


def send_kernel(meta, white_ref, *send_refs):
    for c, send_ref in enumerate(send_refs, 1):
        for j in range(send_ref.shape[0]):
            send_ref[j] = white_ref[meta[j], pl.ds(32 * BEGIN[c], 32 * SPLIT[c]), :]


def pack_kernel(members, pairs, meta, in_ref, *out_refs):
    me = meta[members * pairs]
    for hop, out_ref in zip(HOPS, out_refs, strict=True):
        to = target(me, hop, members)
        for q in range(pairs):
            out_ref[q] = in_ref[meta[to * pairs + q]]


def cross_octet(octet, local, own_refs, part_refs, rows_ref, store):
    pairs = part_refs[0].shape[0]
    depth = 32 * len(own_refs)
    at = pl.ds(pl.multiple_of(octet * 32, 32), 32)
    own = jnp.concatenate([r[at, :] for r in own_refs], 0).astype(jnp.float32)
    halves = own.reshape(depth // 16, 2, 8, BCH)
    turned = jnp.stack([halves[:, 1], -halves[:, 0]], axis=1).reshape(depth, BCH)
    rows_ref[0] = own.T
    rows_ref[1] = turned.T
    at = pl.ds(pl.multiple_of(local * 32, 32), 32)
    right = jnp.concatenate(
        [jnp.concatenate([r[q, at, :] for r in part_refs], 0) for q in range(pairs)], 1
    )
    same = (
        lax.broadcasted_iota(jnp.int32, (8, depth), 0)
        == lax.broadcasted_iota(jnp.int32, (8, depth), 1) % 8
    )
    for i0 in range(0, BCH, 16):
        tiles = []
        for i in range(i0, i0 + 16):
            for v in range(2):
                row = rows_ref[v, pl.ds(i, 8, stride=0), :]
                tiles.append(jnp.where(same, row, 0.0))
        left = jnp.concatenate(tiles, 0).astype(jnp.bfloat16)
        cross = jnp.dot(left, right, preferred_element_type=jnp.float32)
        store(i0, cross.astype(jnp.bfloat16).reshape(16, 16, pairs * BCH))


def cross_kernel(members, begin, *refs):
    own_refs, part_refs = refs[:members], refs[members : 2 * members]
    cross_ref, rows_ref = refs[2 * members :]
    step = pl.program_id(0)

    def store(i0, value):
        cross_ref[0, i0 : i0 + 16] = value

    cross_octet(begin + step, step, own_refs, part_refs, rows_ref, store)


def pair_kernel(members, lag_ref, *refs):
    own_refs, part_refs = refs[:members], refs[members : 2 * members]
    early_refs = refs[2 * members : 2 * members + LAST]
    out_ref, cross_ref, rows_ref, sem = refs[2 * members + LAST :]
    pairs = out_ref.shape[0]
    octets = SPLIT[LAST]
    step = pl.program_id(0)

    def fetch(c, block):
        at = pl.ds(block * 8, 8)
        return pltpu.make_async_copy(
            early_refs[c].at[:, at],
            cross_ref.at[pl.ds(BEGIN[c], SPLIT[c]), at],
            sem.at[c, block],
        )

    @pl.when(step == 0)
    def _():
        for block in range(BCH // 8):
            for c in range(LAST):
                fetch(c, block).start()

    @pl.when(step < octets)
    def _():
        def store(i0, value):
            cross_ref[BEGIN[LAST] + step, i0 : i0 + 16] = value

        cross_octet(BEGIN[LAST] + step, step, own_refs, part_refs, rows_ref, store)

    @pl.when(step >= octets)
    def _():
        block = step - octets
        for c in range(LAST):
            fetch(c, block).wait()
        scale = 1.0 / math.sqrt(members * 2 * BINS)
        for ii in range(8):
            right = cross_ref[:, block * 8 + ii].reshape(2 * BINS, pairs * BCH)
            lagged = jnp.dot(lag_ref[...], right, preferred_element_type=jnp.float32)
            lagged = (lagged * scale).astype(jnp.bfloat16)
            for q in range(pairs):
                out_ref[q, :, ii * BCH : (ii + 1) * BCH] = lagged[:, q * BCH : (q + 1) * BCH]


def params(mib):
    return pltpu.CompilerParams(vmem_limit_bytes=mib * 1024 * 1024)


def bf16(*shape):
    return jax.ShapeDtypeStruct(shape, jnp.bfloat16)


def prefetched(n_in, n_out):
    return pltpu.PrefetchScalarGridSpec(
        num_scalar_prefetch=1, grid=(), in_specs=[IN_VMEM] * n_in, out_specs=[IN_VMEM] * n_out
    )


def correlate(own, parts, early, pairs):
    members = len(own)
    octets = SPLIT[LAST]

    def after(s):
        return jnp.maximum(s - octets, 0)

    return pl.pallas_call(
        functools.partial(pair_kernel, members),
        grid=(octets + BCH // 8,),
        in_specs=[IN_VMEM] * (1 + 2 * members)
        + [pl.BlockSpec(memory_space=pl.ANY)] * LAST,
        out_specs=pl.BlockSpec((pairs, LAGS, 8 * BCH), lambda s: (0, 0, after(s))),
        out_shape=bf16(pairs, LAGS, BCH * BCH),
        scratch_shapes=[
            pltpu.VMEM((OCT, BCH, 16, pairs * BCH), jnp.bfloat16),
            pltpu.VMEM((2, BCH, 32 * members), jnp.float32),
            pltpu.SemaphoreType.DMA((LAST, BCH // 8)),
        ],
        compiler_params=params(44),
        name="correlate",
    )(jnp.asarray(lag_table()), *own, *parts, *early)


def crossed(c, own, parts, pairs):
    members = len(own)
    return pl.pallas_call(
        functools.partial(cross_kernel, members, BEGIN[c]),
        grid=(SPLIT[c],),
        in_specs=[IN_VMEM] * (2 * members),
        out_specs=pl.BlockSpec((1, BCH, 16, pairs * BCH), lambda s: (s, 0, 0, 0)),
        out_shape=bf16(SPLIT[c], BCH, 16, pairs * BCH),
        scratch_shapes=[pltpu.VMEM((2, BCH, 32 * members), jnp.float32)],
        compiler_params=params(20),
        cost_estimate=pl.CostEstimate(
            flops=2_000_000_000 * SPLIT[c], bytes_accessed=2**21 * SPLIT[c], transcendentals=0
        ),
        name="cross",
    )(*own, *parts)


def shards(record, deck_ids, partners):
    groups = lax.axis_size("blk")
    members = lax.axis_size("win")
    group = lax.axis_index("blk")
    member = lax.axis_index("win")
    pairs = partners.shape[1]

    def move(pieces):
        moved = [pieces[0]]
        for (dz, dc), piece in zip(HOPS[1:], pieces[1:], strict=True):
            ring = members // 2
            way = [(m, (m // 2 + dz) % ring * 2 + (m + dc) % 2) for m in range(members)]
            moved.append(lax.ppermute(piece, "win", way))
        return moved

    listed = partners.reshape(groups, members * pairs)
    here = listed // members == group
    first = jnp.min(jnp.where(here, listed % members, members), axis=1)
    second = jnp.max(jnp.where(here, listed % members, -1), axis=1)
    slots = jnp.stack([first, second], axis=1).reshape(-1)
    decks = lax.dynamic_slice_in_dim(deck_ids, group * members, members, 0)
    meta = jnp.concatenate([slots, decks, member.reshape(1)]).astype(jnp.int32)
    wanted = lax.dynamic_slice_in_dim(listed, group, 1, 0).reshape(-1)
    lower = (wanted[None, :] // members == wanted[:, None] // members) & (
        wanted[None, :] < wanted[:, None]
    )
    place = 2 * (wanted // members) + jnp.any(lower, axis=1).astype(jnp.int32)
    place = jnp.concatenate([place, member.reshape(1)]).astype(jnp.int32)

    white_shape = (members, ROWS, BCH)
    send_shapes = [(2 * groups, 32 * n, BCH) for n in SPLIT]
    shapes = [white_shape, send_shapes[0]] + [(ROWS, BCH)] * members
    white, send, *own = pl.pallas_call(
        functools.partial(spectra_kernel, members, groups),
        grid_spec=pltpu.PrefetchScalarGridSpec(
            num_scalar_prefetch=1,
            grid=(members // AT_ONCE,),
            in_specs=[
                pl.BlockSpec((AT_ONCE * BCH, 2 * WS), lambda b, meta: (b, 0)),
                IN_VMEM,
            ],
            out_specs=[IN_VMEM] * len(shapes),
        ),
        out_shape=[bf16(*s) for s in shapes],
        compiler_params=params(16),
        name="spectra",
    )(meta, record, jnp.asarray(forward_table()))
    sends = pl.pallas_call(
        send_kernel,
        grid_spec=prefetched(1, LAST),
        out_shape=[bf16(*s) for s in send_shapes[1:]],
        compiler_params=params(16),
        cost_estimate=pl.CostEstimate(flops=0, bytes_accessed=2**23, transcendentals=0),
        name="send",
    )(meta, white)
    sends = [send, *sends]
    own = move(own)

    early = []
    parts = None
    for c, octets in enumerate(SPLIT):
        got = lax.all_to_all(
            sends[c].reshape(groups, 64 * octets, BCH),
            "blk",
            split_axis=0,
            concat_axis=0,
            tiled=True,
        )
        if c == 0:
            got, own, place = lax.optimization_barrier((got, own, place))
        else:
            got, parts = lax.optimization_barrier((got, parts))
            early.append(crossed(c - 1, own, parts, pairs))
        if c >= 2:
            got, early[c - 2] = lax.optimization_barrier((got, early[c - 2]))
        if c < LAST:
            got, sends[c + 1] = lax.optimization_barrier((got, sends[c + 1]))
        parts = pl.pallas_call(
            functools.partial(pack_kernel, members, pairs),
            grid_spec=prefetched(1, members),
            out_shape=[bf16(pairs, 32 * octets, BCH)] * members,
            compiler_params=params(16),
            name="pack",
        )(place, got.reshape(send_shapes[c]))
        parts = move(parts)
    return correlate(own, parts, early, pairs)


def solution(mesh):
    return jax.shard_map(
        shards,
        mesh=mesh,
        in_specs=(P("blk", "win"), P(), P()),
        out_specs=P(("blk", "win"), None, None),
        check_vma=False,
    )
```

```python
import functools
import math

import jax
import jax.numpy as jnp
import ml_dtypes
import numpy as np
from jax import lax
from jax.experimental import pallas as pl
from jax.experimental.pallas import tpu as pltpu
from jax.sharding import PartitionSpec as P

WS = 512
BINS = 128
LAGS = 64
BCH = 128
OCT = BINS // 8
ROWS = OCT * 32
SPLIT = (8, 8)
BEGIN = tuple(sum(SPLIT[:c]) for c in range(len(SPLIT)))
LAST = len(SPLIT) - 1
AT_ONCE = 4
LAG_BLOCK = 16
HOPS = ((0, 0), (1, 0), (3, 0), (1, 1), (3, 1), (2, 0), (2, 1), (0, 1))
IN_HBM = pl.BlockSpec(memory_space=pltpu.HBM)
IN_VMEM = pl.BlockSpec(memory_space=pltpu.VMEM)


def forward_table():
    t = np.arange(WS)
    f = np.arange(1, BINS + 1)
    angle = (f[:, None] * t[None, :] % WS) * (2.0 * math.pi / WS)
    return np.concatenate([np.cos(angle), -np.sin(angle)], 0).astype(ml_dtypes.bfloat16)


def lag_table():
    f = np.arange(1, BINS + 1)
    s = np.arange(LAGS) - LAGS // 2
    angle = (s[:, None] * f[None, :] % WS) * (2.0 * math.pi / WS)
    both = np.stack([np.cos(angle), -np.sin(angle)], 1).reshape(LAGS, 2, OCT, 8)
    return both.transpose(0, 2, 1, 3).reshape(LAGS, 2 * BINS).astype(ml_dtypes.bfloat16)


def target(me, hop, members):
    z = lax.rem(me // 2 + hop[0], members // 2)
    return 2 * z + lax.rem(me + hop[1], 2)


def spectra_kernel(members, groups, partners, decks, record_ref, factor_ref, *refs):
    send_refs, own_refs = refs[: LAST + 1], refs[LAST + 1 : LAST + 1 + members]
    x_ref, table_ref, white_ref, slots, in_sem, send_sem, own_sem = refs[LAST + 1 + members :]
    group, me = lax.axis_index("blk"), lax.axis_index("win")
    table_copy = pltpu.make_async_copy(factor_ref, table_ref, in_sem.at[members // AT_ONCE])
    table_copy.start()
    copies = []
    for step in range(members // AT_ONCE):
        at = pl.ds(step * AT_ONCE * BCH, AT_ONCE * BCH)
        copies.append(pltpu.make_async_copy(record_ref.at[at], x_ref.at[at], in_sem.at[step]))
        copies[step].start()

    def wanted(g, _):
        low, high = jnp.int32(members), jnp.int32(-1)
        for m in range(members):
            for q in range(partners.shape[0]):
                block = partners[q, g * members + m] - group * members
                here = (block >= 0) & (block < members)
                low = jnp.minimum(low, jnp.where(here, block, members))
                high = jnp.maximum(high, jnp.where(here, block, -1))
        slots[2 * g] = low
        slots[2 * g + 1] = high
        return 0

    lax.fori_loop(0, groups, wanted, 0)
    table_copy.wait()
    for step, copy in enumerate(copies):
        copy.wait()
        first = step * AT_ONCE
        for w in range(2):
            spectra = lax.dot_general(
                table_ref[...],
                x_ref[first * BCH : (first + AT_ONCE) * BCH, w * WS : (w + 1) * WS],
                (((1,), (1,)), ((), ())),
                preferred_element_type=jnp.float32,
            )
            power = jnp.sum(spectra * spectra, axis=0, keepdims=True) / BINS
            root = jnp.sqrt(power + 1e-06)
            for b in range(AT_ONCE):
                at = slice(b * BCH, (b + 1) * BCH)
                deck = decks[group * members + first + b]
                white = spectra[:, at] * ((1.0 - 2.0 * deck.astype(jnp.float32)) / root[:, at])
                for o in range(OCT):
                    tile = jnp.concatenate(
                        [white[o * 8 : o * 8 + 8], white[BINS + o * 8 : BINS + o * 8 + 8]], 0
                    )
                    row = o * 32 + w * 16
                    white_ref[first + b, row : row + 16, :] = tile.astype(jnp.bfloat16)
    copies = []
    for c, send_ref in enumerate(send_refs):
        for j in range(2 * groups):
            piece = white_ref.at[slots[j], pl.ds(32 * BEGIN[c], 32 * SPLIT[c])]
            copies.append(pltpu.make_async_copy(piece, send_ref.at[j], send_sem.at[c, j]))
    for k, hop in enumerate(HOPS):
        piece = white_ref.at[target(me, hop, members)]
        copies.append(pltpu.make_async_copy(piece, own_refs[k], own_sem.at[k]))
    for copy in copies:
        copy.start()
    for copy in copies:
        copy.wait()


def pack_kernel(members, pairs, meta, in_ref, *out_refs):
    me = meta[members * pairs]
    for hop, out_ref in zip(HOPS, out_refs, strict=True):
        to = target(me, hop, members)
        for q in range(pairs):
            out_ref[q] = in_ref[meta[to * pairs + q]]


def cross_octet(octet, local, own_refs, part_refs, rows_ref, store):
    pairs = part_refs[0].shape[0]
    depth = 32 * len(own_refs)
    at = pl.ds(pl.multiple_of(octet * 32, 32), 32)
    own = jnp.concatenate([r[at, :] for r in own_refs], 0).astype(jnp.float32)
    halves = own.reshape(depth // 16, 2, 8, BCH)
    turned = jnp.stack([halves[:, 1], -halves[:, 0]], axis=1).reshape(depth, BCH)
    rows_ref[0] = own.T
    rows_ref[1] = turned.T
    at = pl.ds(pl.multiple_of(local * 32, 32), 32)
    right = jnp.concatenate(
        [jnp.concatenate([r[q, at, :] for r in part_refs], 0) for q in range(pairs)], 1
    )
    same = (
        lax.broadcasted_iota(jnp.int32, (8, depth), 0)
        == lax.broadcasted_iota(jnp.int32, (8, depth), 1) % 8
    )
    for i0 in range(0, BCH, 16):
        tiles = []
        for i in range(i0, i0 + 16):
            for v in range(2):
                row = rows_ref[v, pl.ds(i, 8, stride=0), :]
                tiles.append(jnp.where(same, row, 0.0))
        left = jnp.concatenate(tiles, 0).astype(jnp.bfloat16)
        cross = jnp.dot(left, right, preferred_element_type=jnp.float32)
        store(i0, cross.astype(jnp.bfloat16).reshape(16, 16, pairs * BCH))


def chunk_kernel(c, members, lag_ref, *refs):
    own_refs, part_refs = refs[:members], refs[members : 2 * members]
    before_ref = refs[2 * members] if c else None
    out_ref, cross_ref, rows_ref = refs[-3:]
    pairs = part_refs[0].shape[0]
    octets = SPLIT[c]
    step = pl.program_id(0)

    @pl.when(step < octets)
    def _():
        def store(i0, value):
            cross_ref[step, i0 : i0 + 16] = value

        cross_octet(BEGIN[c] + step, step, own_refs, part_refs, rows_ref, store)

    @pl.when(step >= octets)
    def _():
        scale = 1.0 / math.sqrt(members * 2 * BINS)
        for ii in range(LAG_BLOCK):
            i = (step - octets) * LAG_BLOCK + ii
            right = cross_ref[:, i].reshape(16 * octets, pairs * BCH)
            lagged = jnp.dot(lag_ref[...], right, preferred_element_type=jnp.float32)
            if c:
                lagged = lagged + before_ref[i]
            if c < LAST:
                out_ref[i] = lagged
                continue
            lagged = (lagged * scale).astype(jnp.bfloat16)
            for q in range(pairs):
                out_ref[q, :, ii * BCH : (ii + 1) * BCH] = lagged[:, q * BCH : (q + 1) * BCH]


def params(mib):
    return pltpu.CompilerParams(vmem_limit_bytes=mib * 1024 * 1024)


def bf16(*shape):
    return jax.ShapeDtypeStruct(shape, jnp.bfloat16)


def prefetched(n_in, n_out):
    return pltpu.PrefetchScalarGridSpec(
        num_scalar_prefetch=1, grid=(), in_specs=[IN_VMEM] * n_in, out_specs=[IN_VMEM] * n_out
    )


def chunk(c, own, parts, before, pairs):
    members = len(own)
    octets = SPLIT[c]
    lags = jnp.asarray(lag_table()[:, 16 * BEGIN[c] : 16 * (BEGIN[c] + octets)])
    blocks = BCH // LAG_BLOCK
    if c == LAST:
        out = bf16(pairs, LAGS, BCH * BCH)
        out_spec = pl.BlockSpec(
            (pairs, LAGS, LAG_BLOCK * BCH), lambda s: (0, 0, jnp.maximum(s - octets, 0))
        )
    else:
        out = jax.ShapeDtypeStruct((BCH, LAGS, pairs * BCH), jnp.float32)
        out_spec = IN_VMEM
    return pl.pallas_call(
        functools.partial(chunk_kernel, c, members),
        grid=(octets + blocks,),
        in_specs=[IN_VMEM] * (1 + 2 * members + len(before)),
        out_specs=out_spec,
        out_shape=out,
        scratch_shapes=[
            pltpu.VMEM((octets, BCH, 16, pairs * BCH), jnp.bfloat16),
            pltpu.VMEM((2, BCH, 32 * members), jnp.float32),
        ],
        compiler_params=params(40),
        cost_estimate=pl.CostEstimate(
            flops=2_500_000_000 * octets, bytes_accessed=2**21 * octets, transcendentals=0
        ),
        name="chunk",
    )(lags, *own, *parts, *before)


def shards(record, deck_ids, partners):
    groups = lax.axis_size("blk")
    members = lax.axis_size("win")
    group = lax.axis_index("blk")
    member = lax.axis_index("win")
    pairs = partners.shape[1]

    def move(pieces):
        moved = [pieces[0]]
        for (dz, dc), piece in zip(HOPS[1:], pieces[1:], strict=True):
            ring = members // 2
            way = [(m, (m // 2 + dz) % ring * 2 + (m + dc) % 2) for m in range(members)]
            moved.append(lax.ppermute(piece, "win", way))
        return moved

    listed = partners.reshape(groups, members * pairs)
    wanted = lax.dynamic_slice_in_dim(listed, group, 1, 0).reshape(-1)
    lower = (wanted[None, :] // members == wanted[:, None] // members) & (
        wanted[None, :] < wanted[:, None]
    )
    place = 2 * (wanted // members) + jnp.any(lower, axis=1).astype(jnp.int32)
    place = jnp.concatenate([place, member.reshape(1)]).astype(jnp.int32)

    send_shapes = [(2 * groups, 32 * n, BCH) for n in SPLIT]
    shapes = send_shapes + [(ROWS, BCH)] * members
    outs = pl.pallas_call(
        functools.partial(spectra_kernel, members, groups),
        grid_spec=pltpu.PrefetchScalarGridSpec(
            num_scalar_prefetch=2,
            grid=(),
            in_specs=[IN_HBM] * 2,
            out_specs=[IN_HBM] * len(shapes),
            scratch_shapes=[
                pltpu.VMEM((members * BCH, 2 * WS), jnp.bfloat16),
                pltpu.VMEM((2 * BINS, WS), jnp.bfloat16),
                pltpu.VMEM((members, ROWS, BCH), jnp.bfloat16),
                pltpu.SMEM((2 * groups,), jnp.int32),
                pltpu.SemaphoreType.DMA((members // AT_ONCE + 1,)),
                pltpu.SemaphoreType.DMA((LAST + 1, 2 * groups)),
                pltpu.SemaphoreType.DMA((members,)),
            ],
        ),
        out_shape=[bf16(*s) for s in shapes],
        compiler_params=params(58),
        name="spectra",
    )(partners.T, deck_ids, record, jnp.asarray(forward_table()))
    sends, own = list(outs[: LAST + 1]), list(outs[LAST + 1 :])
    own = move(own)

    before = []
    parts = None
    for c, octets in enumerate(SPLIT):
        got = lax.all_to_all(
            sends[c].reshape(groups, 64 * octets, BCH),
            "blk",
            split_axis=0,
            concat_axis=0,
            tiled=True,
        )
        if c == 0:
            got, own, place = lax.optimization_barrier((got, own, place))
        else:
            got, parts = lax.optimization_barrier((got, parts))
            before = [chunk(c - 1, own, parts, before, pairs)]
        if c < LAST:
            got, sends[c + 1] = lax.optimization_barrier((got, sends[c + 1]))
        parts = pl.pallas_call(
            functools.partial(pack_kernel, members, pairs),
            grid_spec=prefetched(1, members),
            out_shape=[bf16(pairs, 32 * octets, BCH)] * members,
            compiler_params=params(16),
            name="pack",
        )(place, got.reshape(send_shapes[c]))
        parts = move(parts)
    return chunk(LAST, own, parts, before, pairs)


def solution(mesh):
    return jax.shard_map(
        shards,
        mesh=mesh,
        in_specs=(P("blk", "win"), P(), P()),
        out_specs=P(("blk", "win"), None, None),
        check_vma=False,
    )
```

```python
import functools
import math

import jax
import jax.numpy as jnp
import ml_dtypes
import numpy as np
from jax import lax
from jax.experimental import pallas as pl
from jax.experimental.pallas import tpu as pltpu
from jax.sharding import PartitionSpec as P

WS = 512
BINS = 128
LAGS = 64
BCH = 128
OCT = BINS // 8
ROWS = OCT * 32
SPLIT = (8, 8)
BEGIN = tuple(sum(SPLIT[:c]) for c in range(len(SPLIT)))
LAST = len(SPLIT) - 1
AT_ONCE = 4
LAG_BLOCK = 16
HOPS = ((0, 0), (1, 0), (3, 0), (1, 1), (3, 1), (2, 0), (2, 1), (0, 1))
IN_HBM = pl.BlockSpec(memory_space=pltpu.HBM)
IN_VMEM = pl.BlockSpec(memory_space=pltpu.VMEM)


def forward_table():
    t = np.arange(WS)
    f = np.arange(1, BINS + 1)
    angle = (f[:, None] * t[None, :] % WS) * (2.0 * math.pi / WS)
    return np.concatenate([np.cos(angle), -np.sin(angle)], 0).astype(ml_dtypes.bfloat16)


def lag_table():
    f = np.arange(1, BINS + 1)
    s = np.arange(LAGS) - LAGS // 2
    angle = (s[:, None] * f[None, :] % WS) * (2.0 * math.pi / WS)
    both = np.stack([np.cos(angle), -np.sin(angle)], 1).reshape(LAGS, 2, OCT, 8)
    return both.transpose(0, 2, 1, 3).reshape(LAGS, 2 * BINS).astype(ml_dtypes.bfloat16)


def target(me, hop, members):
    z = lax.rem(me // 2 + hop[0], members // 2)
    return 2 * z + lax.rem(me + hop[1], 2)


def spectra_kernel(members, groups, partners, decks, record_ref, factor_ref, *refs):
    send_refs, own_refs = refs[: LAST + 1], refs[LAST + 1 : LAST + 1 + members]
    x_ref, table_ref, white_ref, slots, in_sem, send_sem, own_sem = refs[LAST + 1 + members :]
    group, me = lax.axis_index("blk"), lax.axis_index("win")
    table_copy = pltpu.make_async_copy(factor_ref, table_ref, in_sem.at[members // AT_ONCE])
    table_copy.start()
    copies = []
    for step in range(members // AT_ONCE):
        at = pl.ds(step * AT_ONCE * BCH, AT_ONCE * BCH)
        copies.append(pltpu.make_async_copy(record_ref.at[at], x_ref.at[at], in_sem.at[step]))
        copies[step].start()

    def wanted(g, _):
        low, high = jnp.int32(members), jnp.int32(-1)
        for m in range(members):
            for q in range(partners.shape[0]):
                block = partners[q, g * members + m] - group * members
                here = (block >= 0) & (block < members)
                low = jnp.minimum(low, jnp.where(here, block, members))
                high = jnp.maximum(high, jnp.where(here, block, -1))
        slots[2 * g] = low
        slots[2 * g + 1] = high
        return 0

    lax.fori_loop(0, groups, wanted, 0)
    table_copy.wait()
    for step, copy in enumerate(copies):
        copy.wait()
        first = step * AT_ONCE
        for w in range(2):
            spectra = lax.dot_general(
                table_ref[...],
                x_ref[first * BCH : (first + AT_ONCE) * BCH, w * WS : (w + 1) * WS],
                (((1,), (1,)), ((), ())),
                preferred_element_type=jnp.float32,
            )
            power = jnp.sum(spectra * spectra, axis=0, keepdims=True) / BINS
            root = jnp.sqrt(power + 1e-06)
            for b in range(AT_ONCE):
                at = slice(b * BCH, (b + 1) * BCH)
                deck = decks[group * members + first + b]
                white = spectra[:, at] * ((1.0 - 2.0 * deck.astype(jnp.float32)) / root[:, at])
                for o in range(OCT):
                    tile = jnp.concatenate(
                        [white[o * 8 : o * 8 + 8], white[BINS + o * 8 : BINS + o * 8 + 8]], 0
                    )
                    row = o * 32 + w * 16
                    white_ref[first + b, row : row + 16, :] = tile.astype(jnp.bfloat16)
    copies = []
    for c, send_ref in enumerate(send_refs):
        for j in range(2 * groups):
            piece = white_ref.at[slots[j], pl.ds(32 * BEGIN[c], 32 * SPLIT[c])]
            copies.append(pltpu.make_async_copy(piece, send_ref.at[j], send_sem.at[c, j]))
    for k, hop in enumerate(HOPS):
        piece = white_ref.at[target(me, hop, members)]
        copies.append(pltpu.make_async_copy(piece, own_refs[k], own_sem.at[k]))
    for copy in copies:
        copy.start()
    for copy in copies:
        copy.wait()


def pack_kernel(members, pairs, meta, in_ref, *out_refs):
    me = meta[members * pairs]
    for hop, out_ref in zip(HOPS, out_refs, strict=True):
        to = target(me, hop, members)
        for q in range(pairs):
            out_ref[q] = in_ref[meta[to * pairs + q]]


def cross_octet(octet, local, own_refs, part_refs, rows_ref, store):
    pairs = part_refs[0].shape[0]
    depth = 32 * len(own_refs)
    at = pl.ds(pl.multiple_of(octet * 32, 32), 32)
    own = jnp.concatenate([r[at, :] for r in own_refs], 0).astype(jnp.float32)
    halves = own.reshape(depth // 16, 2, 8, BCH)
    turned = jnp.stack([halves[:, 1], -halves[:, 0]], axis=1).reshape(depth, BCH)
    rows_ref[0] = own.T
    rows_ref[1] = turned.T
    at = pl.ds(pl.multiple_of(local * 32, 32), 32)
    right = jnp.concatenate(
        [jnp.concatenate([r[q, at, :] for r in part_refs], 0) for q in range(pairs)], 1
    )
    same = (
        lax.broadcasted_iota(jnp.int32, (8, depth), 0)
        == lax.broadcasted_iota(jnp.int32, (8, depth), 1) % 8
    )
    for i0 in range(0, BCH, 16):
        tiles = []
        for i in range(i0, i0 + 16):
            for v in range(2):
                row = rows_ref[v, pl.ds(i, 8, stride=0), :]
                tiles.append(jnp.where(same, row, 0.0))
        left = jnp.concatenate(tiles, 0).astype(jnp.bfloat16)
        cross = jnp.dot(left, right, preferred_element_type=jnp.float32)
        store(i0, cross.astype(jnp.bfloat16).reshape(16, 16, pairs * BCH))


def chunk_kernel(c, members, lag_ref, *refs):
    own_refs, part_refs = refs[:members], refs[members : 2 * members]
    refs = refs[2 * members :]
    if c:
        before_ref, out_ref, cross_ref, rows_ref, held_ref, sem = refs
    else:
        out_ref, cross_ref, rows_ref = refs
    pairs = part_refs[0].shape[0]
    octets = SPLIT[c]
    step = pl.program_id(0)

    def fetch(block):
        at = pl.ds(block * LAG_BLOCK, LAG_BLOCK)
        return pltpu.make_async_copy(before_ref.at[at], held_ref.at[at], sem.at[block])

    if c:

        @pl.when(step == 0)
        def _():
            for block in range(BCH // LAG_BLOCK):
                fetch(block).start()

    @pl.when(step < octets)
    def _():
        def store(i0, value):
            cross_ref[step, i0 : i0 + 16] = value

        cross_octet(BEGIN[c] + step, step, own_refs, part_refs, rows_ref, store)

    @pl.when(step >= octets)
    def _():
        scale = 1.0 / math.sqrt(members * 2 * BINS)
        if c:
            fetch(step - octets).wait()
        for ii in range(LAG_BLOCK):
            i = (step - octets) * LAG_BLOCK + ii
            right = cross_ref[:, i].reshape(16 * octets, pairs * BCH)
            lagged = jnp.dot(lag_ref[...], right, preferred_element_type=jnp.float32)
            if c:
                lagged = lagged + held_ref[i]
            if c < LAST:
                out_ref[ii] = lagged
                continue
            lagged = (lagged * scale).astype(jnp.bfloat16)
            for q in range(pairs):
                out_ref[q, :, ii * BCH : (ii + 1) * BCH] = lagged[:, q * BCH : (q + 1) * BCH]


def params(mib):
    return pltpu.CompilerParams(vmem_limit_bytes=mib * 1024 * 1024)


def bf16(*shape):
    return jax.ShapeDtypeStruct(shape, jnp.bfloat16)


def prefetched(n_in, n_out):
    return pltpu.PrefetchScalarGridSpec(
        num_scalar_prefetch=1, grid=(), in_specs=[IN_VMEM] * n_in, out_specs=[IN_VMEM] * n_out
    )


def chunk(c, own, parts, before, pairs):
    members = len(own)
    octets = SPLIT[c]
    lags = jnp.asarray(lag_table()[:, 16 * BEGIN[c] : 16 * (BEGIN[c] + octets)])
    blocks = BCH // LAG_BLOCK
    sums = (BCH, LAGS, pairs * BCH)

    def after(s):
        return jnp.maximum(s - octets, 0)

    if c == LAST:
        out = bf16(pairs, LAGS, BCH * BCH)
        out_spec = pl.BlockSpec((pairs, LAGS, LAG_BLOCK * BCH), lambda s: (0, 0, after(s)))
    else:
        out = jax.ShapeDtypeStruct(sums, jnp.float32)
        out_spec = pl.BlockSpec((LAG_BLOCK, *sums[1:]), lambda s: (after(s), 0, 0))
    held = [pltpu.VMEM(sums, jnp.float32), pltpu.SemaphoreType.DMA((blocks,))] if c else []
    return pl.pallas_call(
        functools.partial(chunk_kernel, c, members),
        grid=(octets + blocks,),
        in_specs=[IN_VMEM] * (1 + 2 * members) + [IN_HBM] * len(before),
        out_specs=out_spec,
        out_shape=out,
        scratch_shapes=[
            pltpu.VMEM((octets, BCH, 16, pairs * BCH), jnp.bfloat16),
            pltpu.VMEM((2, BCH, 32 * members), jnp.float32),
            *held,
        ],
        compiler_params=params(48),
        cost_estimate=pl.CostEstimate(
            flops=2_500_000_000 * octets, bytes_accessed=2**21 * octets, transcendentals=0
        ),
        name="chunk",
    )(lags, *own, *parts, *before)


def shards(record, deck_ids, partners):
    groups = lax.axis_size("blk")
    members = lax.axis_size("win")
    group = lax.axis_index("blk")
    member = lax.axis_index("win")
    pairs = partners.shape[1]

    def move(pieces):
        moved = [pieces[0]]
        for (dz, dc), piece in zip(HOPS[1:], pieces[1:], strict=True):
            ring = members // 2
            way = [(m, (m // 2 + dz) % ring * 2 + (m + dc) % 2) for m in range(members)]
            moved.append(lax.ppermute(piece, "win", way))
        return moved

    listed = partners.reshape(groups, members * pairs)
    wanted = lax.dynamic_slice_in_dim(listed, group, 1, 0).reshape(-1)
    lower = (wanted[None, :] // members == wanted[:, None] // members) & (
        wanted[None, :] < wanted[:, None]
    )
    place = 2 * (wanted // members) + jnp.any(lower, axis=1).astype(jnp.int32)
    place = jnp.concatenate([place, member.reshape(1)]).astype(jnp.int32)

    send_shapes = [(2 * groups, 32 * n, BCH) for n in SPLIT]
    shapes = send_shapes + [(ROWS, BCH)] * members
    outs = pl.pallas_call(
        functools.partial(spectra_kernel, members, groups),
        grid_spec=pltpu.PrefetchScalarGridSpec(
            num_scalar_prefetch=2,
            grid=(),
            in_specs=[IN_HBM] * 2,
            out_specs=[IN_HBM] * len(shapes),
            scratch_shapes=[
                pltpu.VMEM((members * BCH, 2 * WS), jnp.bfloat16),
                pltpu.VMEM((2 * BINS, WS), jnp.bfloat16),
                pltpu.VMEM((members, ROWS, BCH), jnp.bfloat16),
                pltpu.SMEM((2 * groups,), jnp.int32),
                pltpu.SemaphoreType.DMA((members // AT_ONCE + 1,)),
                pltpu.SemaphoreType.DMA((LAST + 1, 2 * groups)),
                pltpu.SemaphoreType.DMA((members,)),
            ],
        ),
        out_shape=[bf16(*s) for s in shapes],
        compiler_params=params(58),
        name="spectra",
    )(partners.T, deck_ids, record, jnp.asarray(forward_table()))
    sends, own = list(outs[: LAST + 1]), list(outs[LAST + 1 :])
    own = move(own)

    before = []
    parts = None
    for c, octets in enumerate(SPLIT):
        got = lax.all_to_all(
            sends[c].reshape(groups, 64 * octets, BCH),
            "blk",
            split_axis=0,
            concat_axis=0,
            tiled=True,
        )
        if c == 0:
            got, own, place = lax.optimization_barrier((got, own, place))
        else:
            got, parts = lax.optimization_barrier((got, parts))
            before = [chunk(c - 1, own, parts, before, pairs)]
        if c < LAST:
            got, sends[c + 1] = lax.optimization_barrier((got, sends[c + 1]))
        parts = pl.pallas_call(
            functools.partial(pack_kernel, members, pairs),
            grid_spec=prefetched(1, members),
            out_shape=[bf16(pairs, 32 * octets, BCH)] * members,
            compiler_params=params(16),
            name="pack",
        )(place, got.reshape(send_shapes[c]))
        parts = move(parts)
    return chunk(LAST, own, parts, before, pairs)


def solution(mesh):
    return jax.shard_map(
        shards,
        mesh=mesh,
        in_specs=(P("blk", "win"), P(), P()),
        out_specs=P(("blk", "win"), None, None),
        check_vma=False,
    )
```

```python
import functools
import math

import jax
import jax.numpy as jnp
import ml_dtypes
import numpy as np
from jax import lax
from jax.experimental import pallas as pl
from jax.experimental.pallas import tpu as pltpu
from jax.sharding import PartitionSpec as P

WS = 512
BINS = 128
LAGS = 64
BCH = 128
OCT = BINS // 8
ROWS = OCT * 32
SPLIT = (8, 8)
BEGIN = tuple(sum(SPLIT[:c]) for c in range(len(SPLIT)))
LAST = len(SPLIT) - 1
AT_ONCE = 4
LAG_BLOCK = 32
HOPS = ((0, 0), (1, 0), (3, 0), (2, 0), (1, 1), (3, 1), (2, 1), (0, 1))
IN_HBM = pl.BlockSpec(memory_space=pltpu.HBM)
IN_VMEM = pl.BlockSpec(memory_space=pltpu.VMEM)


def forward_table():
    t = np.arange(WS)
    f = np.arange(1, BINS + 1)
    angle = (f[:, None] * t[None, :] % WS) * (2.0 * math.pi / WS)
    return np.concatenate([np.cos(angle), -np.sin(angle)], 0).astype(ml_dtypes.bfloat16)


def lag_table():
    f = np.arange(1, BINS + 1)
    s = np.arange(LAGS) - LAGS // 2
    angle = (s[:, None] * f[None, :] % WS) * (2.0 * math.pi / WS)
    both = np.stack([np.cos(angle), -np.sin(angle)], 1).reshape(LAGS, 2, OCT, 8)
    return both.transpose(0, 2, 1, 3).reshape(LAGS, 2 * BINS).astype(ml_dtypes.bfloat16)


def target(me, hop, members):
    z = lax.rem(me // 2 + hop[0], members // 2)
    return 2 * z + lax.rem(me + hop[1], 2)


def spectra_kernel(members, groups, partners, decks, record_ref, factor_ref, *refs):
    send_refs, own_refs = refs[: LAST + 1], refs[LAST + 1 : LAST + 1 + members]
    x_ref, table_ref, white_ref, slots, in_sem, send_sem, own_sem = refs[LAST + 1 + members :]
    group, me = lax.axis_index("blk"), lax.axis_index("win")
    table_copy = pltpu.make_async_copy(factor_ref, table_ref, in_sem.at[members // AT_ONCE])
    table_copy.start()
    copies = []
    for step in range(members // AT_ONCE):
        at = pl.ds(step * AT_ONCE * BCH, AT_ONCE * BCH)
        copies.append(pltpu.make_async_copy(record_ref.at[at], x_ref.at[at], in_sem.at[step]))
        copies[step].start()

    def wanted(g, _):
        low, high = jnp.int32(members), jnp.int32(-1)
        for m in range(members):
            for q in range(partners.shape[0]):
                block = partners[q, g * members + m] - group * members
                here = (block >= 0) & (block < members)
                low = jnp.minimum(low, jnp.where(here, block, members))
                high = jnp.maximum(high, jnp.where(here, block, -1))
        slots[2 * g] = low
        slots[2 * g + 1] = high
        return 0

    lax.fori_loop(0, groups, wanted, 0)
    table_copy.wait()
    for step, copy in enumerate(copies):
        copy.wait()
        first = step * AT_ONCE
        for w in range(2):
            spectra = lax.dot_general(
                table_ref[...],
                x_ref[first * BCH : (first + AT_ONCE) * BCH, w * WS : (w + 1) * WS],
                (((1,), (1,)), ((), ())),
                preferred_element_type=jnp.float32,
            )
            power = jnp.sum(spectra * spectra, axis=0, keepdims=True) / BINS
            root = jnp.sqrt(power + 1e-06)
            for b in range(AT_ONCE):
                at = slice(b * BCH, (b + 1) * BCH)
                deck = decks[group * members + first + b]
                white = spectra[:, at] * ((1.0 - 2.0 * deck.astype(jnp.float32)) / root[:, at])
                for o in range(OCT):
                    tile = jnp.concatenate(
                        [white[o * 8 : o * 8 + 8], white[BINS + o * 8 : BINS + o * 8 + 8]], 0
                    )
                    row = o * 32 + w * 16
                    white_ref[first + b, row : row + 16, :] = tile.astype(jnp.bfloat16)
    copies = []
    for c, send_ref in enumerate(send_refs):
        for j in range(2 * groups):
            piece = white_ref.at[slots[j], pl.ds(32 * BEGIN[c], 32 * SPLIT[c])]
            copies.append(pltpu.make_async_copy(piece, send_ref.at[j], send_sem.at[c, j]))
    for k, hop in enumerate(HOPS):
        piece = white_ref.at[target(me, hop, members)]
        copies.append(pltpu.make_async_copy(piece, own_refs[k], own_sem.at[k]))
    for copy in copies:
        copy.start()
    for copy in copies:
        copy.wait()


def pack_kernel(members, pairs, meta, in_ref, *out_refs):
    me = meta[members * pairs]
    for hop, out_ref in zip(HOPS, out_refs, strict=True):
        to = target(me, hop, members)
        for q in range(pairs):
            out_ref[q] = in_ref[meta[to * pairs + q]]


def cross_octet(octet, local, own_refs, part_refs, rows_ref, store):
    pairs = part_refs[0].shape[0]
    depth = 32 * len(own_refs)
    at = pl.ds(pl.multiple_of(octet * 32, 32), 32)
    own = jnp.concatenate([r[at, :] for r in own_refs], 0).astype(jnp.float32)
    halves = own.reshape(depth // 16, 2, 8, BCH)
    turned = jnp.stack([halves[:, 1], -halves[:, 0]], axis=1).reshape(depth, BCH)
    rows_ref[0] = own.T
    rows_ref[1] = turned.T
    at = pl.ds(pl.multiple_of(local * 32, 32), 32)
    right = jnp.concatenate(
        [jnp.concatenate([r[q, at, :] for r in part_refs], 0) for q in range(pairs)], 1
    )
    same = (
        lax.broadcasted_iota(jnp.int32, (8, depth), 0)
        == lax.broadcasted_iota(jnp.int32, (8, depth), 1) % 8
    )
    for i0 in range(0, BCH, 16):
        tiles = []
        for i in range(i0, i0 + 16):
            for v in range(2):
                row = rows_ref[v, pl.ds(i, 8, stride=0), :]
                tiles.append(jnp.where(same, row, 0.0))
        left = jnp.concatenate(tiles, 0).astype(jnp.bfloat16)
        cross = jnp.dot(left, right, preferred_element_type=jnp.float32)
        store(i0, cross.astype(jnp.bfloat16).reshape(16, 16, pairs * BCH))


def chunk_kernel(c, members, lag_ref, *refs):
    own_refs, part_refs = refs[:members], refs[members : 2 * members]
    refs = refs[2 * members :]
    if c:
        before_ref, out_ref, cross_ref, rows_ref = refs
    else:
        out_ref, cross_ref, rows_ref = refs
    pairs = part_refs[0].shape[0]
    octets = SPLIT[c]
    step = pl.program_id(0)

    @pl.when(step < octets)
    def _():
        def store(i0, value):
            cross_ref[step, i0 : i0 + 16] = value

        cross_octet(BEGIN[c] + step, step, own_refs, part_refs, rows_ref, store)

    @pl.when(step >= octets)
    def _():
        scale = 1.0 / math.sqrt(members * 2 * BINS)
        for ii in range(LAG_BLOCK):
            i = (step - octets) * LAG_BLOCK + ii
            right = cross_ref[:, i].reshape(16 * octets, pairs * BCH)
            lagged = jnp.dot(lag_ref[...], right, preferred_element_type=jnp.float32)
            if c:
                lagged = lagged + before_ref[i]
            if c < LAST:
                out_ref[i] = lagged
                continue
            lagged = (lagged * scale).astype(jnp.bfloat16)
            for q in range(pairs):
                out_ref[q, :, ii * BCH : (ii + 1) * BCH] = lagged[:, q * BCH : (q + 1) * BCH]


def params(mib):
    return pltpu.CompilerParams(vmem_limit_bytes=mib * 1024 * 1024)


def bf16(*shape):
    return jax.ShapeDtypeStruct(shape, jnp.bfloat16)


def chunk(c, own, parts, before, pairs):
    members = len(own)
    octets = SPLIT[c]
    lags = jnp.asarray(lag_table()[:, 16 * BEGIN[c] : 16 * (BEGIN[c] + octets)])
    blocks = BCH // LAG_BLOCK
    sums = (BCH, LAGS, pairs * BCH)

    def after(s):
        return jnp.maximum(s - octets, 0)

    if c == LAST:
        out = bf16(pairs, LAGS, BCH * BCH)
        out_spec = pl.BlockSpec((pairs, LAGS, LAG_BLOCK * BCH), lambda s: (0, 0, after(s)))
    else:
        out = jax.ShapeDtypeStruct(sums, jnp.float32)
        out_spec = IN_VMEM
    return pl.pallas_call(
        functools.partial(chunk_kernel, c, members),
        grid=(octets + blocks,),
        in_specs=[IN_VMEM] * (1 + 2 * members + len(before)),
        out_specs=out_spec,
        out_shape=out,
        scratch_shapes=[
            pltpu.VMEM((octets, BCH, 16, pairs * BCH), jnp.bfloat16),
            pltpu.VMEM((2, BCH, 32 * members), jnp.float32),
        ],
        compiler_params=params(22),
        cost_estimate=pl.CostEstimate(
            flops=2_500_000_000 * octets, bytes_accessed=2**21 * octets, transcendentals=0
        ),
        name="chunk",
    )(lags, *own, *parts, *before)


def shards(record, deck_ids, partners):
    groups = lax.axis_size("blk")
    members = lax.axis_size("win")
    group = lax.axis_index("blk")
    member = lax.axis_index("win")
    pairs = partners.shape[1]

    def move(pieces):
        moved = [pieces[0]]
        for (dz, dc), piece in zip(HOPS[1:], pieces[1:], strict=True):
            ring = members // 2
            way = [(m, (m // 2 + dz) % ring * 2 + (m + dc) % 2) for m in range(members)]
            moved.append(lax.ppermute(piece, "win", way))
        return moved

    listed = partners.reshape(groups, members * pairs)
    wanted = lax.dynamic_slice_in_dim(listed, group, 1, 0).reshape(-1)
    lower = (wanted[None, :] // members == wanted[:, None] // members) & (
        wanted[None, :] < wanted[:, None]
    )
    place = 2 * (wanted // members) + jnp.any(lower, axis=1).astype(jnp.int32)
    place = jnp.concatenate([place, member.reshape(1)]).astype(jnp.int32)

    send_shapes = [(2 * groups, 32 * n, BCH) for n in SPLIT]
    shapes = send_shapes + [(ROWS, BCH)] * members
    outs = pl.pallas_call(
        functools.partial(spectra_kernel, members, groups),
        grid_spec=pltpu.PrefetchScalarGridSpec(
            num_scalar_prefetch=2,
            grid=(),
            in_specs=[IN_HBM] * 2,
            out_specs=[IN_HBM] * len(shapes),
            scratch_shapes=[
                pltpu.VMEM((members * BCH, 2 * WS), jnp.bfloat16),
                pltpu.VMEM((2 * BINS, WS), jnp.bfloat16),
                pltpu.VMEM((members, ROWS, BCH), jnp.bfloat16),
                pltpu.SMEM((2 * groups,), jnp.int32),
                pltpu.SemaphoreType.DMA((members // AT_ONCE + 1,)),
                pltpu.SemaphoreType.DMA((LAST + 1, 2 * groups)),
                pltpu.SemaphoreType.DMA((members,)),
            ],
        ),
        out_shape=[bf16(*s) for s in shapes],
        compiler_params=params(58),
        name="spectra",
    )(partners.T, deck_ids, record, jnp.asarray(forward_table()))
    sends, own = list(outs[: LAST + 1]), list(outs[LAST + 1 :])
    own = move(own)

    before = []
    parts = None
    for c, octets in enumerate(SPLIT):
        got = lax.all_to_all(
            sends[c].reshape(groups, 64 * octets, BCH),
            "blk",
            split_axis=0,
            concat_axis=0,
            tiled=True,
        )
        if c == 0:
            got, own, place = lax.optimization_barrier((got, own, place))
        else:
            got, parts = lax.optimization_barrier((got, parts))
            before = [chunk(c - 1, own, parts, before, pairs)]
        if c < LAST:
            got, sends[c + 1] = lax.optimization_barrier((got, sends[c + 1]))
        parts = pl.pallas_call(
            functools.partial(pack_kernel, members, pairs),
            grid_spec=pltpu.PrefetchScalarGridSpec(
                num_scalar_prefetch=1,
                grid=(),
                in_specs=[IN_VMEM],
                out_specs=[IN_VMEM] * members,
            ),
            out_shape=[bf16(pairs, 32 * octets, BCH)] * members,
            compiler_params=params(16),
            name="pack",
        )(place, got.reshape(send_shapes[c]))
        parts = move(parts)
    return chunk(LAST, own, parts, before, pairs)


def solution(mesh):
    return jax.shard_map(
        shards,
        mesh=mesh,
        in_specs=(P("blk", "win"), P(), P()),
        out_specs=P(("blk", "win"), None, None),
        check_vma=False,
    )
```

```python
import functools
import math

import jax
import jax.numpy as jnp
import ml_dtypes
import numpy as np
from jax import lax
from jax.experimental import pallas as pl
from jax.experimental.pallas import tpu as pltpu
from jax.sharding import PartitionSpec as P

WS = 512
BINS = 128
LAGS = 64
BCH = 128
OCT = BINS // 8
ROWS = OCT * 32
SPLIT = (8, 8)
BEGIN = tuple(sum(SPLIT[:c]) for c in range(len(SPLIT)))
LAST = len(SPLIT) - 1
AT_ONCE = 8
AT_STEP = 4
LAG_BLOCK = 32
HOPS = ((0, 0), (1, 0), (3, 0), (2, 0), (1, 1), (3, 1), (2, 1), (0, 1))
IN_HBM = pl.BlockSpec(memory_space=pltpu.HBM)
IN_VMEM = pl.BlockSpec(memory_space=pltpu.VMEM)


def forward_table():
    t = np.arange(WS)
    f = np.arange(1, BINS + 1)
    angle = (f[:, None] * t[None, :] % WS) * (2.0 * math.pi / WS)
    return np.concatenate([np.cos(angle), -np.sin(angle)], 0).astype(ml_dtypes.bfloat16)


def lag_table():
    f = np.arange(1, BINS + 1)
    s = np.arange(LAGS) - LAGS // 2
    angle = (s[:, None] * f[None, :] % WS) * (2.0 * math.pi / WS)
    both = np.stack([np.cos(angle), -np.sin(angle)], 1).reshape(LAGS, 2, OCT, 8)
    return both.transpose(0, 2, 1, 3).reshape(LAGS, 2 * BINS).astype(ml_dtypes.bfloat16)


def target(me, hop, members):
    z = lax.rem(me // 2 + hop[0], members // 2)
    return 2 * z + lax.rem(me + hop[1], 2)


def spectra_kernel(members, groups, partners, decks, record_ref, factor_ref, *refs):
    send_refs, own_refs = refs[: LAST + 1], refs[LAST + 1 : LAST + 1 + members]
    x_ref, table_ref, white_ref, slots, in_sem, send_sem, own_sem = refs[LAST + 1 + members :]
    group, me = lax.axis_index("blk"), lax.axis_index("win")
    table_copy = pltpu.make_async_copy(factor_ref, table_ref, in_sem.at[members // AT_ONCE])
    table_copy.start()
    copies = []
    for step in range(members // AT_ONCE):
        at = pl.ds(step * AT_ONCE * BCH, AT_ONCE * BCH)
        copies.append(pltpu.make_async_copy(record_ref.at[at], x_ref.at[at], in_sem.at[step]))
        copies[step].start()

    def wanted(g, _):
        low, high = jnp.int32(members), jnp.int32(-1)
        for m in range(members):
            for q in range(partners.shape[0]):
                block = partners[q, g * members + m] - group * members
                here = (block >= 0) & (block < members)
                low = jnp.minimum(low, jnp.where(here, block, members))
                high = jnp.maximum(high, jnp.where(here, block, -1))
        slots[2 * g] = low
        slots[2 * g + 1] = high
        return 0

    lax.fori_loop(0, groups, wanted, 0)
    table_copy.wait()
    for step, copy in enumerate(copies):
        copy.wait()
        first = step * AT_ONCE
        for w in range(2):
            spectra = lax.dot_general(
                table_ref[...],
                x_ref[first * BCH : (first + AT_ONCE) * BCH, w * WS : (w + 1) * WS],
                (((1,), (1,)), ((), ())),
                preferred_element_type=jnp.float32,
            )
            power = jnp.sum(spectra * spectra, axis=0, keepdims=True) / BINS
            root = jnp.sqrt(power + 1e-06)
            for b in range(AT_ONCE):
                at = slice(b * BCH, (b + 1) * BCH)
                deck = decks[group * members + first + b]
                white = spectra[:, at] * ((1.0 - 2.0 * deck.astype(jnp.float32)) / root[:, at])
                for o in range(OCT):
                    tile = jnp.concatenate(
                        [white[o * 8 : o * 8 + 8], white[BINS + o * 8 : BINS + o * 8 + 8]], 0
                    )
                    row = o * 32 + w * 16
                    white_ref[first + b, row : row + 16, :] = tile.astype(jnp.bfloat16)
    copies = []
    for c, send_ref in enumerate(send_refs):
        for j in range(2 * groups):
            piece = white_ref.at[slots[j], pl.ds(32 * BEGIN[c], 32 * SPLIT[c])]
            copies.append(pltpu.make_async_copy(piece, send_ref.at[j], send_sem.at[c, j]))
    for k, hop in enumerate(HOPS):
        piece = white_ref.at[target(me, hop, members)]
        copies.append(pltpu.make_async_copy(piece, own_refs[k], own_sem.at[k]))
    for copy in copies:
        copy.start()
    for copy in copies:
        copy.wait()


def pack_kernel(members, pairs, meta, in_ref, *out_refs):
    me = meta[members * pairs]
    for hop, out_ref in zip(HOPS, out_refs, strict=True):
        to = target(me, hop, members)
        for q in range(pairs):
            out_ref[q] = in_ref[meta[to * pairs + q]]


def cross_octet(octet, local, own_refs, part_refs, rows_ref, store):
    pairs = part_refs[0].shape[0]
    depth = 32 * len(own_refs)
    at = pl.ds(pl.multiple_of(octet * 32, 32), 32)
    own = jnp.concatenate([r[at, :] for r in own_refs], 0).astype(jnp.float32)
    halves = own.reshape(depth // 16, 2, 8, BCH)
    turned = jnp.stack([halves[:, 1], -halves[:, 0]], axis=1).reshape(depth, BCH)
    rows_ref[0] = own.T
    rows_ref[1] = turned.T
    at = pl.ds(pl.multiple_of(local * 32, 32), 32)
    right = jnp.concatenate(
        [jnp.concatenate([r[q, at, :] for r in part_refs], 0) for q in range(pairs)], 1
    )
    same = (
        lax.broadcasted_iota(jnp.int32, (8, depth), 0)
        == lax.broadcasted_iota(jnp.int32, (8, depth), 1) % 8
    )
    for i0 in range(0, BCH, 16):
        tiles = []
        for i in range(i0, i0 + 16):
            for v in range(2):
                row = rows_ref[v, pl.ds(i, 8, stride=0), :]
                tiles.append(jnp.where(same, row, 0.0))
        left = jnp.concatenate(tiles, 0).astype(jnp.bfloat16)
        cross = jnp.dot(left, right, preferred_element_type=jnp.float32)
        store(i0, cross.astype(jnp.bfloat16).reshape(16, 16, pairs * BCH))


def chunk_kernel(c, members, lag_ref, *refs):
    own_refs, part_refs = refs[:members], refs[members : 2 * members]
    refs = refs[2 * members :]
    if c:
        before_ref, out_ref, cross_ref, rows_ref, *refs = refs
    else:
        out_ref, cross_ref, rows_ref, *refs = refs
    pairs = part_refs[0].shape[0]
    octets = SPLIT[c]
    step = pl.program_id(0)
    turns = octets // AT_STEP

    if c == LAST:
        made_ref, sem = refs

    def give(part):
        at = pl.ds(pl.multiple_of(part * 8 * BCH, 8 * BCH), 8 * BCH)
        return pltpu.make_async_copy(made_ref.at[:, :, at], out_ref.at[:, :, at], sem.at[part])

    @pl.when(step < turns)
    def _():
        for n in range(AT_STEP):
            local = step * AT_STEP + n

            def store(i0, value, local=local):
                cross_ref[local, i0 : i0 + 16] = value

            cross_octet(BEGIN[c] + local, local, own_refs, part_refs, rows_ref.at[n], store)

    @pl.when(step >= turns)
    def _():
        scale = 1.0 / math.sqrt(members * 2 * BINS)
        for ii in range(LAG_BLOCK):
            i = (step - turns) * LAG_BLOCK + ii
            right = cross_ref[:, i].reshape(16 * octets, pairs * BCH)
            lagged = jnp.dot(lag_ref[...], right, preferred_element_type=jnp.float32)
            if c:
                lagged = lagged + before_ref[i]
            if c < LAST:
                out_ref[i] = lagged
                continue
            lagged = (lagged * scale).astype(jnp.bfloat16)
            at = pl.ds(pl.multiple_of(i * BCH, BCH), BCH)
            for q in range(pairs):
                made_ref[q, :, at] = lagged[:, q * BCH : (q + 1) * BCH]
            if ii % 8 == 7:
                give(i // 8).start()

    if c == LAST:

        @pl.when(step == turns + BCH // LAG_BLOCK - 1)
        def _():
            for part in range(BCH // 8):
                give(part).wait()


def params(mib):
    return pltpu.CompilerParams(vmem_limit_bytes=mib * 1024 * 1024)


def bf16(*shape):
    return jax.ShapeDtypeStruct(shape, jnp.bfloat16)


def chunk(c, own, parts, before, pairs):
    members = len(own)
    octets = SPLIT[c]
    lags = jnp.asarray(lag_table()[:, 16 * BEGIN[c] : 16 * (BEGIN[c] + octets)])
    blocks = BCH // LAG_BLOCK
    sums = (BCH, LAGS, pairs * BCH)

    if c == LAST:
        out = bf16(pairs, LAGS, BCH * BCH)
        made = [pltpu.VMEM(out.shape, jnp.bfloat16), pltpu.SemaphoreType.DMA((BCH // 8,))]
    else:
        out = jax.ShapeDtypeStruct(sums, jnp.float32)
        made = []
    return pl.pallas_call(
        functools.partial(chunk_kernel, c, members),
        grid=(octets // AT_STEP + blocks,),
        in_specs=[IN_VMEM] * (1 + 2 * members + len(before)),
        out_specs=IN_HBM if c == LAST else IN_VMEM,
        out_shape=out,
        scratch_shapes=[
            pltpu.VMEM((octets, BCH, 16, pairs * BCH), jnp.bfloat16),
            pltpu.VMEM((AT_STEP, 2, BCH, 32 * members), jnp.float32),
            *made,
        ],
        compiler_params=params(28),
        cost_estimate=pl.CostEstimate(
            flops=2_500_000_000 * octets, bytes_accessed=2**21 * octets, transcendentals=0
        ),
        name="chunk",
    )(lags, *own, *parts, *before)


def shards(record, deck_ids, partners):
    groups = lax.axis_size("blk")
    members = lax.axis_size("win")
    group = lax.axis_index("blk")
    member = lax.axis_index("win")
    pairs = partners.shape[1]

    def move(pieces):
        moved = [pieces[0]]
        for (dz, dc), piece in zip(HOPS[1:], pieces[1:], strict=True):
            ring = members // 2
            way = [(m, (m // 2 + dz) % ring * 2 + (m + dc) % 2) for m in range(members)]
            moved.append(lax.ppermute(piece, "win", way))
        return moved

    listed = partners.reshape(groups, members * pairs)
    wanted = lax.dynamic_slice_in_dim(listed, group, 1, 0).reshape(-1)
    lower = (wanted[None, :] // members == wanted[:, None] // members) & (
        wanted[None, :] < wanted[:, None]
    )
    place = 2 * (wanted // members) + jnp.any(lower, axis=1).astype(jnp.int32)
    place = jnp.concatenate([place, member.reshape(1)]).astype(jnp.int32)

    send_shapes = [(2 * groups, 32 * n, BCH) for n in SPLIT]
    shapes = send_shapes + [(ROWS, BCH)] * members
    outs = pl.pallas_call(
        functools.partial(spectra_kernel, members, groups),
        grid_spec=pltpu.PrefetchScalarGridSpec(
            num_scalar_prefetch=2,
            grid=(),
            in_specs=[IN_HBM] * 2,
            out_specs=[IN_HBM] * len(shapes),
            scratch_shapes=[
                pltpu.VMEM((members * BCH, 2 * WS), jnp.bfloat16),
                pltpu.VMEM((2 * BINS, WS), jnp.bfloat16),
                pltpu.VMEM((members, ROWS, BCH), jnp.bfloat16),
                pltpu.SMEM((2 * groups,), jnp.int32),
                pltpu.SemaphoreType.DMA((members // AT_ONCE + 1,)),
                pltpu.SemaphoreType.DMA((LAST + 1, 2 * groups)),
                pltpu.SemaphoreType.DMA((members,)),
            ],
        ),
        out_shape=[bf16(*s) for s in shapes],
        compiler_params=params(58),
        name="spectra",
    )(partners.T, deck_ids, record, jnp.asarray(forward_table()))
    sends, own = list(outs[: LAST + 1]), list(outs[LAST + 1 :])
    own = move(own)

    before = []
    parts = None
    for c, octets in enumerate(SPLIT):
        got = lax.all_to_all(
            sends[c].reshape(groups, 64 * octets, BCH),
            "blk",
            split_axis=0,
            concat_axis=0,
            tiled=True,
        )
        if c == 0:
            got, own, place = lax.optimization_barrier((got, own, place))
        else:
            got, parts = lax.optimization_barrier((got, parts))
            before = [chunk(c - 1, own, parts, before, pairs)]
        if c < LAST:
            got, sends[c + 1] = lax.optimization_barrier((got, sends[c + 1]))
        parts = pl.pallas_call(
            functools.partial(pack_kernel, members, pairs),
            grid_spec=pltpu.PrefetchScalarGridSpec(
                num_scalar_prefetch=1,
                grid=(),
                in_specs=[IN_VMEM],
                out_specs=[IN_VMEM] * members,
            ),
            out_shape=[bf16(pairs, 32 * octets, BCH)] * members,
            compiler_params=params(16),
            name="pack",
        )(place, got.reshape(send_shapes[c]))
        parts = move(parts)
    return chunk(LAST, own, parts, before, pairs)


def solution(mesh):
    return jax.shard_map(
        shards,
        mesh=mesh,
        in_specs=(P("blk", "win"), P(), P()),
        out_specs=P(("blk", "win"), None, None),
        check_vma=False,
    )
```

```python
import functools
import math

import jax
import jax.numpy as jnp
import ml_dtypes
import numpy as np
from jax import lax
from jax.experimental import pallas as pl
from jax.experimental.pallas import tpu as pltpu
from jax.sharding import PartitionSpec as P

WS = 512
BINS = 128
LAGS = 64
BCH = 128
OCT = BINS // 8
ROWS = OCT * 32
SPLIT = (8, 8)
BEGIN = tuple(sum(SPLIT[:c]) for c in range(len(SPLIT)))
LAST = len(SPLIT) - 1
AT_ONCE = 8
AT_STEP = 4
LAG_BLOCK = 32
HOPS = ((0, 0), (1, 0), (3, 0), (2, 0), (1, 1), (3, 1), (2, 1), (0, 1))
IN_HBM = pl.BlockSpec(memory_space=pltpu.HBM)
IN_VMEM = pl.BlockSpec(memory_space=pltpu.VMEM)


def forward_table():
    t = np.arange(WS)
    f = np.arange(1, BINS + 1)
    angle = (f[:, None] * t[None, :] % WS) * (2.0 * math.pi / WS)
    return np.concatenate([np.cos(angle), -np.sin(angle)], 0).astype(ml_dtypes.bfloat16)


def lag_table():
    f = np.arange(1, BINS + 1)
    s = np.arange(LAGS) - LAGS // 2
    angle = (s[:, None] * f[None, :] % WS) * (2.0 * math.pi / WS)
    both = np.stack([np.cos(angle), -np.sin(angle)], 1).reshape(LAGS, 2, OCT, 8)
    return both.transpose(0, 2, 1, 3).reshape(LAGS, 2 * BINS).astype(ml_dtypes.bfloat16)


def target(me, hop, members):
    z = lax.rem(me // 2 + hop[0], members // 2)
    return 2 * z + lax.rem(me + hop[1], 2)


def spectra_kernel(members, groups, partners, decks, record_ref, factor_ref, *refs):
    send_refs, own_refs = refs[: LAST + 1], refs[LAST + 1 : LAST + 1 + members]
    x_ref, table_ref, white_ref, slots, in_sem, send_sem, own_sem = refs[LAST + 1 + members :]
    group, me = lax.axis_index("blk"), lax.axis_index("win")
    table_copy = pltpu.make_async_copy(factor_ref, table_ref, in_sem.at[members // AT_ONCE])
    table_copy.start()
    copies = []
    for step in range(members // AT_ONCE):
        at = pl.ds(step * AT_ONCE * BCH, AT_ONCE * BCH)
        copies.append(pltpu.make_async_copy(record_ref.at[at], x_ref.at[at], in_sem.at[step]))
        copies[step].start()

    def wanted(g, _):
        low, high = jnp.int32(members), jnp.int32(-1)
        for m in range(members):
            for q in range(partners.shape[0]):
                block = partners[q, g * members + m] - group * members
                here = (block >= 0) & (block < members)
                low = jnp.minimum(low, jnp.where(here, block, members))
                high = jnp.maximum(high, jnp.where(here, block, -1))
        slots[2 * g] = low
        slots[2 * g + 1] = high
        return 0

    lax.fori_loop(0, groups, wanted, 0)
    table_copy.wait()
    for step, copy in enumerate(copies):
        copy.wait()
        first = step * AT_ONCE
        for w in range(2):
            spectra = lax.dot_general(
                table_ref[...],
                x_ref[first * BCH : (first + AT_ONCE) * BCH, w * WS : (w + 1) * WS],
                (((1,), (1,)), ((), ())),
                preferred_element_type=jnp.float32,
            )
            power = jnp.sum(spectra * spectra, axis=0, keepdims=True) / BINS
            root = jnp.sqrt(power + 1e-06)
            for b in range(AT_ONCE):
                at = slice(b * BCH, (b + 1) * BCH)
                deck = decks[group * members + first + b]
                white = spectra[:, at] * ((1.0 - 2.0 * deck.astype(jnp.float32)) / root[:, at])
                for o in range(OCT):
                    tile = jnp.concatenate(
                        [white[o * 8 : o * 8 + 8], white[BINS + o * 8 : BINS + o * 8 + 8]], 0
                    )
                    row = o * 32 + w * 16
                    white_ref[first + b, row : row + 16, :] = tile.astype(jnp.bfloat16)
    copies = []
    for c, send_ref in enumerate(send_refs):
        for j in range(2 * groups):
            piece = white_ref.at[slots[j], pl.ds(32 * BEGIN[c], 32 * SPLIT[c])]
            copies.append(pltpu.make_async_copy(piece, send_ref.at[j], send_sem.at[c, j]))
    for k, hop in enumerate(HOPS):
        piece = white_ref.at[target(me, hop, members)]
        copies.append(pltpu.make_async_copy(piece, own_refs[k], own_sem.at[k]))
    for copy in copies:
        copy.start()
    for copy in copies:
        copy.wait()


def pack_kernel(members, pairs, meta, in_ref, *out_refs):
    me = meta[members * pairs]
    for hop, out_ref in zip(HOPS, out_refs, strict=True):
        to = target(me, hop, members)
        for q in range(pairs):
            out_ref[q] = in_ref[meta[to * pairs + q]]


def cross_octet(octet, local, own_refs, part_refs, rows_ref, store):
    pairs = part_refs[0].shape[0]
    depth = 32 * len(own_refs)
    at = pl.ds(pl.multiple_of(octet * 32, 32), 32)
    own = jnp.concatenate([r[at, :] for r in own_refs], 0).astype(jnp.float32)
    halves = own.reshape(depth // 16, 2, 8, BCH)
    turned = jnp.stack([halves[:, 1], -halves[:, 0]], axis=1).reshape(depth, BCH)
    rows_ref[0, :BCH] = own.T
    rows_ref[1, :BCH] = turned.T
    at = pl.ds(pl.multiple_of(local * 32, 32), 32)
    right = jnp.concatenate(
        [jnp.concatenate([r[q, at, :] for r in part_refs], 0) for q in range(pairs)], 1
    )
    same = (
        lax.broadcasted_iota(jnp.int32, (8, depth), 0)
        == lax.broadcasted_iota(jnp.int32, (8, depth), 1) % 8
    )
    for i0 in range(0, BCH, 16):
        tiles = []
        for i in range(i0, i0 + 16):
            for v in range(2):
                row = rows_ref[v, pl.ds(i, 8, stride=0), :]
                tiles.append(jnp.where(same, row, 0.0))
        left = jnp.concatenate(tiles, 0).astype(jnp.bfloat16)
        cross = jnp.dot(left, right, preferred_element_type=jnp.float32)
        store(i0, cross.astype(jnp.bfloat16).reshape(16, 16, pairs * BCH))


def chunk_kernel(c, members, lag_ref, *refs):
    own_refs, part_refs = refs[:members], refs[members : 2 * members]
    refs = refs[2 * members :]
    if c:
        before_ref, out_ref, cross_ref, rows_ref, *refs = refs
    else:
        out_ref, cross_ref, rows_ref, *refs = refs
    pairs = part_refs[0].shape[0]
    octets = SPLIT[c]
    step = pl.program_id(0)
    turns = octets // AT_STEP

    if c == LAST:
        made_ref, sem = refs

    def give(part):
        at = pl.ds(pl.multiple_of(part * 8 * BCH, 8 * BCH), 8 * BCH)
        return pltpu.make_async_copy(made_ref.at[:, :, at], out_ref.at[:, :, at], sem.at[part])

    @pl.when(step < turns)
    def _():
        for n in range(AT_STEP):
            local = step * AT_STEP + n

            def store(i0, value, local=local):
                cross_ref[local, i0 : i0 + 16] = value

            cross_octet(BEGIN[c] + local, local, own_refs, part_refs, rows_ref.at[n], store)

    @pl.when(step >= turns)
    def _():
        scale = 1.0 / math.sqrt(members * 2 * BINS)
        for ii in range(LAG_BLOCK):
            i = (step - turns) * LAG_BLOCK + ii
            right = cross_ref[:, i].reshape(16 * octets, pairs * BCH)
            lagged = jnp.dot(lag_ref[...], right, preferred_element_type=jnp.float32)
            if c:
                lagged = lagged + before_ref[i]
            if c < LAST:
                out_ref[i] = lagged
                continue
            lagged = (lagged * scale).astype(jnp.bfloat16)
            at = pl.ds(pl.multiple_of(i * BCH, BCH), BCH)
            for q in range(pairs):
                made_ref[q, :, at] = lagged[:, q * BCH : (q + 1) * BCH]
            if ii % 8 == 7:
                give(i // 8).start()

    if c == LAST:

        @pl.when(step == turns + BCH // LAG_BLOCK - 1)
        def _():
            for part in range(BCH // 8):
                give(part).wait()


def params(mib):
    return pltpu.CompilerParams(vmem_limit_bytes=mib * 1024 * 1024)


def bf16(*shape):
    return jax.ShapeDtypeStruct(shape, jnp.bfloat16)


def chunk(c, own, parts, before, pairs):
    members = len(own)
    octets = SPLIT[c]
    lags = jnp.asarray(lag_table()[:, 16 * BEGIN[c] : 16 * (BEGIN[c] + octets)])
    blocks = BCH // LAG_BLOCK
    sums = (BCH, LAGS, pairs * BCH)

    if c == LAST:
        out = bf16(pairs, LAGS, BCH * BCH)
        made = [pltpu.VMEM(out.shape, jnp.bfloat16), pltpu.SemaphoreType.DMA((BCH // 8,))]
    else:
        out = jax.ShapeDtypeStruct(sums, jnp.float32)
        made = []
    return pl.pallas_call(
        functools.partial(chunk_kernel, c, members),
        grid=(octets // AT_STEP + blocks,),
        in_specs=[IN_VMEM] * (1 + 2 * members + len(before)),
        out_specs=IN_HBM if c == LAST else IN_VMEM,
        out_shape=out,
        scratch_shapes=[
            pltpu.VMEM((octets, BCH, 16, pairs * BCH), jnp.bfloat16),
            pltpu.VMEM((AT_STEP, 2, BCH + 8, 32 * members), jnp.float32),
            *made,
        ],
        compiler_params=params(28),
        cost_estimate=pl.CostEstimate(
            flops=2_500_000_000 * octets, bytes_accessed=2**21 * octets, transcendentals=0
        ),
        name="chunk",
    )(lags, *own, *parts, *before)


def shards(record, deck_ids, partners):
    groups = lax.axis_size("blk")
    members = lax.axis_size("win")
    group = lax.axis_index("blk")
    member = lax.axis_index("win")
    pairs = partners.shape[1]

    def move(pieces):
        moved = [pieces[0]]
        for (dz, dc), piece in zip(HOPS[1:], pieces[1:], strict=True):
            ring = members // 2
            way = [(m, (m // 2 + dz) % ring * 2 + (m + dc) % 2) for m in range(members)]
            moved.append(lax.ppermute(piece, "win", way))
        return moved

    listed = partners.reshape(groups, members * pairs)
    wanted = lax.dynamic_slice_in_dim(listed, group, 1, 0).reshape(-1)
    lower = (wanted[None, :] // members == wanted[:, None] // members) & (
        wanted[None, :] < wanted[:, None]
    )
    place = 2 * (wanted // members) + jnp.any(lower, axis=1).astype(jnp.int32)
    place = jnp.concatenate([place, member.reshape(1)]).astype(jnp.int32)

    send_shapes = [(2 * groups, 32 * n, BCH) for n in SPLIT]
    shapes = send_shapes + [(ROWS, BCH)] * members
    outs = pl.pallas_call(
        functools.partial(spectra_kernel, members, groups),
        grid_spec=pltpu.PrefetchScalarGridSpec(
            num_scalar_prefetch=2,
            grid=(),
            in_specs=[IN_HBM] * 2,
            out_specs=[IN_HBM] * len(shapes),
            scratch_shapes=[
                pltpu.VMEM((members * BCH, 2 * WS), jnp.bfloat16),
                pltpu.VMEM((2 * BINS, WS), jnp.bfloat16),
                pltpu.VMEM((members, ROWS, BCH), jnp.bfloat16),
                pltpu.SMEM((2 * groups,), jnp.int32),
                pltpu.SemaphoreType.DMA((members // AT_ONCE + 1,)),
                pltpu.SemaphoreType.DMA((LAST + 1, 2 * groups)),
                pltpu.SemaphoreType.DMA((members,)),
            ],
        ),
        out_shape=[bf16(*s) for s in shapes],
        compiler_params=params(58),
        name="spectra",
    )(partners.T, deck_ids, record, jnp.asarray(forward_table()))
    sends, own = list(outs[: LAST + 1]), list(outs[LAST + 1 :])
    own = move(own)

    before = []
    parts = None
    for c, octets in enumerate(SPLIT):
        got = lax.all_to_all(
            sends[c].reshape(groups, 64 * octets, BCH),
            "blk",
            split_axis=0,
            concat_axis=0,
            tiled=True,
        )
        if c == 0:
            got, own, place = lax.optimization_barrier((got, own, place))
        else:
            got, parts = lax.optimization_barrier((got, parts))
            before = [chunk(c - 1, own, parts, before, pairs)]
        if c < LAST:
            got, sends[c + 1] = lax.optimization_barrier((got, sends[c + 1]))
        parts = pl.pallas_call(
            functools.partial(pack_kernel, members, pairs),
            grid_spec=pltpu.PrefetchScalarGridSpec(
                num_scalar_prefetch=1,
                grid=(),
                in_specs=[IN_VMEM],
                out_specs=[IN_VMEM] * members,
            ),
            out_shape=[bf16(pairs, 32 * octets, BCH)] * members,
            compiler_params=params(16),
            name="pack",
        )(place, got.reshape(send_shapes[c]))
        parts = move(parts)
    return chunk(LAST, own, parts, before, pairs)


def solution(mesh):
    return jax.shard_map(
        shards,
        mesh=mesh,
        in_specs=(P("blk", "win"), P(), P()),
        out_specs=P(("blk", "win"), None, None),
        check_vma=False,
    )
```
